32 devices in a mesh: dp: 8 (over y, x, core), chan: 4 (over z).
Axes of the slice: x: 2, y: 2, z: 4, core: 2. Of those that a mesh axis runs over, the one named last changes fastest.
Arguments:
- clips_in: bfloat16 [128, 256, 512], P('dp', None, 'chan'), may hold values from -6 to 6
- speaker: int32 [128], P('dp'), may hold values from 0 to 63
- counts: int32 [8], P('dp'), may hold values from 4 to 16, as said below
- conv_weight: bfloat16 [7, 512], P(None, 'chan'), may hold values from -2 to 2
- conv_bias: bfloat16 [512], P('chan'), may hold values from -1.5 to 1.5
- scale_table: bfloat16 [64, 512], P(None, 'chan'), may hold values from 0.099609375 to 1.8984375
- shift_table: bfloat16 [64, 512], P(None, 'chan'), may hold values from -1.5 to 1.5
- w_in: bfloat16 [512, 1536], P(None, 'chan'), may hold values from -0.25 to 0.25
- b_in: bfloat16 [1536], P('chan'), may hold values from -2.5 to 2.5
- w_out: bfloat16 [1536, 512], P('chan'), may hold values from -0.21875 to 0.21875
- b_out: bfloat16 [512], P('chan'), may hold values from -1.5 to 1.5
- layer_scale: bfloat16 [512], P('chan'), may hold values from 0.5 to 1.5
- grad_out: bfloat16 [128, 256, 512], P('dp', None, 'chan'), may hold values from -6 to 6
Outputs:
- clips_out: bfloat16 [128, 256, 512], P('dp', None, 'chan')
- grad_clips: float32 [128, 256, 512], P('dp', None, 'chan')
- grad_conv_weight: float32 [7, 512], P(None, 'chan')
- grad_conv_bias: float32 [512], P('chan')
- grad_scale_table: float32 [64, 512], P(None, 'chan')
- grad_shift_table: float32 [64, 512], P(None, 'chan')
- grad_w_in: float32 [512, 1536], P(None, 'chan')
- grad_b_in: float32 [1536], P('chan')
- grad_w_out: float32 [1536, 512], P('chan')
- grad_b_out: float32 [512], P('chan')
- grad_layer_scale: float32 [512], P('chan')
The draws below stay inside these ranges and needn't reach their ends.
Inputs may be any that keep to these rules, and one draw needn't show every extreme that they name: `counts`: each index of dp holds 16 clip slots; the slots below its count are live clips, the rest padding. Some index has all 16 slots live.
All inputs are finite; a program needn't handle non-finite values.
Results may differ from the reference program's by a relative error of at most 0.0063.
Values may be sent and summed in bfloat16 or wider, within the bound.
No kernel may reach another device: no remote copies, remote signals or barrier semaphores. Data moves between devices by JAX's collectives and lax.ppermute only.
A program may use at most 128 MiB of HBM per device.

```python
import jax
import jax.numpy as jnp
from jax import lax

D = 512
FF = 1536
KERNEL = 7
LEN = 256
SPK = 64
CLIPS_DEV = 16
CLIPS = 128
N_DP = 8


def draw_counts(key, part):
    drawn_counts = jax.random.randint(key, (N_DP,), max(1, CLIPS_DEV // 4), CLIPS_DEV + 1)
    chosen = jax.random.randint(jax.random.fold_in(key, 7), (), 0, N_DP)
    return jnp.where(jnp.arange(N_DP) == chosen, CLIPS_DEV, drawn_counts).astype(jnp.int32)


def plant(drawn, rng, low, top_value):
    place = [jax.random.randint(jax.random.fold_in(rng, axis), (), 0, length) for axis, length in enumerate(drawn.shape)]
    longest = drawn.shape.index(max(drawn.shape))
    next_to = place[:longest] + [(place[longest] + 1) % drawn.shape[longest]] + place[longest + 1:]
    return drawn.at[tuple(place)].set(low).at[tuple(next_to)].set(top_value)


def block_levels(key, dims, cuts, least, top_value):
    level, own = 1.0, jax.random.fold_in(key, 6)
    for dim, blocks in cuts:
        heights = jnp.exp(jax.random.uniform(jax.random.fold_in(own, dim), (blocks,), jnp.float32, least / len(cuts), top_value / len(cuts)))
        level = level * jnp.repeat(heights, dims[dim] // blocks).reshape([-1 if axis == dim else 1 for axis in range(len(dims))])
    return level


def centred(key, extent, scale, reach, cuts=(), dtype=jnp.bfloat16):
    loudness = block_levels(key, extent, cuts, -0.22, 0.18) if cuts else 1.0
    entries = jax.random.normal(key, extent, jnp.float32) * scale * loudness
    return jnp.minimum(jnp.maximum(entries, -reach), reach).astype(dtype)


def setup_inputs(seed: int = 0) -> dict:
    key_of = jax.random.split(jax.random.key(seed), 14)
    return {
        "clips_in": centred(key_of[0], (CLIPS, LEN, D), 1.0, 6.0, ((0, 8), (2, 4))),
        "speaker": plant(jax.random.randint(key_of[1], (CLIPS,), 0, SPK), jax.random.fold_in(key_of[1], 1), 0, SPK - 1).astype(jnp.int32),
        "counts": draw_counts(jax.random.fold_in(key_of[13], 71), 0),
        "conv_weight": centred(key_of[3], (KERNEL, D), KERNEL ** -0.5, 2.0, ((1, 4),)),
        "conv_bias": centred(key_of[4], (D,), 0.3, 1.5, ((0, 4),)),
        "scale_table": jnp.clip(1.0 + 0.18 * jax.random.normal(key_of[5], (SPK, D), jnp.float32), 0.099609375, 1.8984375).astype(jnp.bfloat16),
        "shift_table": centred(key_of[6], (SPK, D), 0.3, 1.5, ((1, 4),)),
        "w_in": centred(key_of[7], (D, FF), D ** -0.5, 0.25, ((1, 4),)),
        "b_in": centred(key_of[8], (FF,), 0.5, 2.5, ((0, 4),)),
        "w_out": centred(key_of[9], (FF, D), (FF // 2) ** -0.5, 0.21875, ((0, 4),)),
        "b_out": centred(key_of[10], (D,), 0.3, 1.5, ((0, 4),)),
        "layer_scale": jnp.clip(0.5 + 1.0 * jax.random.uniform(key_of[11], (D,), jnp.float32) ** block_levels(key_of[11], (D,), ((0, 4),), -0.2, 0.2), 0.5, 1.5).astype(jnp.bfloat16),
        "grad_out": centred(key_of[12], (CLIPS, LEN, D), 1.0, 6.0, ((0, 8), (2, 4))),
    }


@jax.custom_vjp
def low(v):
    return lax.optimization_barrier(v.astype(jnp.bfloat16)).astype(jnp.float32)

@jax.custom_vjp
def low_back(v):
    return v

def low_keep(v):
    return (low(v), None)

def low_pass(kept, grad):
    return (grad,)

def back_keep(v):
    return (v, None)

def back_low(kept, grad):
    return (low(grad),)
low.defvjp(low_keep, low_pass)
low_back.defvjp(back_keep, back_low)
epsilon = 1e-06
root_half = 0.7071067811865476

def gelu_value(values):
    return 0.5 * values * (1.0 + jax.scipy.special.erf(values * root_half))

def forward(inputs, conv_weight, conv_bias, scale_table, shift_table, w_in, b_in, w_out, b_out, layer_scale, speaker_ids, live):
    clip_num, length, chan_width = inputs.shape
    tap_count = conv_weight.shape[0]
    margin = tap_count // 2
    padded = jnp.pad(inputs, ((0, 0), (margin, margin), (0, 0)))
    conv_out = conv_bias + sum((conv_weight[offset] * padded[:, offset:offset + length] for offset in range(tap_count)))
    row_mean = lax.optimization_barrier(jnp.mean(conv_out, axis=-1, keepdims=True))
    centered = conv_out - row_mean
    variance = lax.optimization_barrier(jnp.mean(centered * centered, axis=-1, keepdims=True))
    normed = centered * lax.rsqrt(variance + epsilon)
    clip_scale = scale_table[speaker_ids][:, None, :]
    clip_shift = shift_table[speaker_ids][:, None, :]
    norm_rows = low(normed * clip_scale + clip_shift).reshape(clip_num * length, chan_width)
    pre_act = low_back(jnp.dot(norm_rows, w_in, precision=lax.Precision.HIGHEST)) + b_in
    act = low(gelu_value(pre_act))
    branch = low_back(jnp.dot(act, w_out, precision=lax.Precision.HIGHEST)) + b_out
    branch = branch.reshape(clip_num, length, chan_width)
    return inputs + branch * layer_scale * live[:, None, None]

def reference(clips_in, speaker, counts, conv_weight, conv_bias, scale_table, shift_table, w_in, b_in, w_out, b_out, layer_scale, grad_out):
    params = (conv_weight.astype(jnp.float32), conv_bias.astype(jnp.float32), scale_table.astype(jnp.float32), shift_table.astype(jnp.float32), w_in.astype(jnp.float32), b_in.astype(jnp.float32), w_out.astype(jnp.float32), b_out.astype(jnp.float32), layer_scale.astype(jnp.float32))
    grouped_in = clips_in.astype(jnp.float32).reshape(N_DP, CLIPS_DEV, LEN, D)
    grouped_grad = grad_out.astype(jnp.float32).reshape(N_DP, CLIPS_DEV, LEN, D)
    grouped_spk = speaker.reshape(N_DP, CLIPS_DEV)

    def per_device(running, item):
        block_in, block_grad, block_spk, live_count = item
        live = (jnp.arange(CLIPS_DEV) < live_count).astype(jnp.float32)

        def apply_block(inputs, *weights):
            return forward(inputs, *weights, block_spk, live)
        result, pull_back = jax.vjp(apply_block, block_in, *params)
        grads = pull_back(block_grad)
        running = tuple((total_now + addend for total_now, addend in zip(running, grads[1:])))
        return (running, (result.astype(jnp.bfloat16), grads[0]))
    initial = tuple((jnp.zeros_like(param) for param in params))
    totals, (results, input_grads) = lax.scan(per_device, initial, (grouped_in, grouped_grad, grouped_spk, counts))
    return (results.reshape(CLIPS, LEN, D), input_grads.reshape(CLIPS, LEN, D), totals[0], totals[1], totals[2], totals[3], totals[4], totals[5], totals[6], totals[7], totals[8])
```

```python
import functools

import jax
import jax.numpy as jnp
from jax import lax
from jax.experimental import pallas as pl
from jax.experimental.pallas import tpu as pltpu
from jax.sharding import PartitionSpec as P

CHUNKS = 1

EPS = 1e-06
ROOT_TWO_PI = 2.5066282746310002
F32 = jnp.float32
BF16 = jnp.bfloat16
PAD = 8


def gelu_pair(v):
    z = jnp.abs(v)
    t = 1.0 / (1.0 + (0.3275911 * 0.7071067811865476) * z)
    e = jnp.exp(v * v * -0.5)
    poly = t * (0.5 * 0.254829592 + t * (0.5 * -0.284496736 + t * (0.5 * 1.421413741 + t * (0.5 * -1.453152027 + t * (0.5 * 1.061405429)))))
    tail = poly * e
    cdf = jnp.where(v >= 0.0, 1.0 - tail, tail)
    return v * cdf, cdf + v * (e * (1.0 / ROOT_TWO_PI))


def dot(a, b, ca, cb):
    return lax.dot_general(a, b, (((ca,), (cb,)), ((), ())), preferred_element_type=F32)


def body(n_blocks, taps, speakers, first,
         order_ref, spk_ref, live_ref, *refs):
    nb = n_blocks
    p = refs[:nb]
    prm, w_in, w_out = refs[nb:nb + 3]
    k = nb + 3
    if not first:
        got = refs[k:k + 3]
        k += 3
    o = refs[k:k + nb]
    gwi, gwo, gsm, grow = refs[k + nb:k + nb + 4]
    (xpad, gpad, normed, nlow, blow, act, slope, plow, wide, b_in) = refs[k + nb + 4:]
    i = pl.program_id(0)
    length, lanes = normed.shape[1], normed.shape[2]
    width = nb * lanes
    ff = act.shape[1]
    per = ff // nb
    margin = taps // 2
    r_conv, r_cb = 2 * speakers, 2 * speakers + taps
    r_bo, r_ls, r_bi = r_cb + 1, r_cb + 2, r_cb + 3
    cols = [pl.multiple_of(order_ref[d] * lanes, lanes) for d in range(nb)]

    @pl.when(i == 0)
    def _():
        for d in range(nb):
            zero = jnp.zeros((PAD, lanes), F32)
            xpad[d, 0:PAD, :] = zero
            xpad[d, PAD + length:, :] = zero
            gpad[d, 0:PAD, :] = zero
            gpad[d, PAD + length:, :] = zero
            for r in range(per // lanes):
                at = pl.multiple_of(order_ref[d] * per + r * lanes, lanes)
                b_in[:, pl.ds(at, lanes)] = prm[d, r_bi + r:r_bi + r + 1, :]
        if first:
            gwi[...] = jnp.zeros_like(gwi)
            gwo[...] = jnp.zeros_like(gwo)
            gsm[...] = jnp.zeros_like(gsm)
        else:
            gwi[...] = got[0][...]
            gwo[...] = got[1][...]
            gsm[...] = got[2][...]

    spk = spk_ref[i]
    live = live_ref[i].astype(F32)
    total = jnp.zeros((length, 1), F32)
    for d in range(nb):
        xpad[d, PAD:PAD + length, :] = p[d][0, 0].astype(F32)
        acc = jnp.broadcast_to(prm[d, r_cb:r_cb + 1, :], (length, lanes))
        for t in range(taps):
            s = PAD - margin + t
            acc = acc + prm[d, r_conv + t:r_conv + t + 1, :] * xpad[d, s:s + length, :]
        normed[d] = acc
        total = total + jnp.sum(acc, 1, keepdims=True)
    mean = total / width
    square = jnp.zeros((length, 1), F32)
    for d in range(nb):
        c = normed[d] - mean
        normed[d] = c
        square = square + jnp.sum(c * c, 1, keepdims=True)
    inv = lax.rsqrt(square / width + EPS)
    for d in range(nb):
        v = normed[d] * inv
        normed[d] = v
        sc = prm[d, pl.ds(spk, 1), :]
        sh = prm[d, pl.ds(speakers + spk, 1), :]
        nlow[:, pl.ds(cols[d], lanes)] = (v * sc + sh).astype(BF16)

    step = 256
    for f in range(0, ff, step):
        pre = dot(nlow[...], w_in[:, f:f + step], 1, 0) + b_in[:, f:f + step]
        a, s = gelu_pair(pre)
        act[:, f:f + step] = a.astype(BF16)
        slope[:, f:f + step] = s
    wide[...] = dot(act[...], w_out[...], 1, 0)
    for d in range(nb):
        b = wide[:, pl.ds(cols[d], lanes)] + prm[d, r_bo:r_bo + 1, :]
        ls = prm[d, r_ls:r_ls + 1, :] * live
        x = p[d][0, 0].astype(F32)
        g = p[d][1, 0].astype(F32)
        o[d][0, 0] = (x + b * ls).astype(BF16)
        gb = g * ls
        gsm[d, taps + 1:taps + 2, :] += jnp.sum(gb, 0, keepdims=True)
        gsm[d, taps + 2:taps + 3, :] += jnp.sum(g * b, 0, keepdims=True) * live
        blow[:, pl.ds(cols[d], lanes)] = gb.astype(BF16)
    for f in range(0, ff, step):
        gp = dot(blow[...], w_out[f:f + step, :], 1, 1) * slope[:, f:f + step]
        low = gp.astype(BF16)
        plow[:, f:f + step] = low
        at = f // lanes
        gsum = jnp.sum(gp, 0, keepdims=True)
        for r in range(step // lanes):
            q = (f + r * lanes) // lanes
            row = taps + 3 + q % (per // lanes)
            gsm[q // (per // lanes) + nb, row:row + 1, :] += gsum[:, r * lanes:(r + 1) * lanes]
        da = dot(nlow[...], low, 0, 0)
        db = dot(blow[...], act[:, f:f + step], 0, 0)
        for r in range(step // lanes):
            gwi[at + r] += da[:, r * lanes:(r + 1) * lanes]
            gwo[at + r] += db[:, r * lanes:(r + 1) * lanes]
    wide[...] = dot(plow[...], w_in[...], 1, 1)
    m1 = jnp.zeros((length, 1), F32)
    m2 = jnp.zeros((length, 1), F32)
    for d in range(nb):
        gn = wide[:, pl.ds(cols[d], lanes)]
        v = normed[d]
        gv = gn * v
        grow[d, pl.ds(i, 1), :] = jnp.sum(gv, 0, keepdims=True)
        grow[d + nb, pl.ds(i, 1), :] = jnp.sum(gn, 0, keepdims=True)
        sc = prm[d, pl.ds(spk, 1), :]
        m1 = m1 + jnp.sum(gn * sc, 1, keepdims=True)
        m2 = m2 + jnp.sum(gv * sc, 1, keepdims=True)
    m1 = m1 / width
    m2 = m2 / width
    for d in range(nb):
        sc = prm[d, pl.ds(spk, 1), :]
        gc = (wide[:, pl.ds(cols[d], lanes)] * sc - m1 - normed[d] * m2) * inv
        gpad[d, PAD:PAD + length, :] = gc
        gsm[d, taps:taps + 1, :] += jnp.sum(gc, 0, keepdims=True)
        acc = jnp.zeros((length, lanes), F32)
        for t in range(taps):
            s = PAD - margin + t
            gsm[d, t:t + 1, :] += jnp.sum(xpad[d, s:s + length, :] * gc, 0, keepdims=True)
            s = PAD + margin - t
            acc = acc + prm[d, r_conv + t:r_conv + t + 1, :] * gpad[d, s:s + length, :]
        o[d][1, 0] = acc.astype(BF16)


def block_call(order, spk, live, packed, prm, w_in, w_out, taps, speakers, carried=None):
    nb = len(packed)
    _, n, length, lanes = packed[0].shape
    width = nb * lanes
    ff = w_in.shape[1]
    rows = 16
    first = carried is None
    full = lambda shape: pl.BlockSpec(shape, lambda i, *_: (0,) * len(shape), pipeline_mode=pl.Buffered(1))
    fullo = lambda shape: pl.BlockSpec(shape, lambda i, *_: (0,) * len(shape))
    pspec = pl.BlockSpec((2, 1, length, lanes), lambda i, *_: (0, i, 0, 0))
    in_specs = [pspec] * nb + [full(prm.shape), full(w_in.shape), full(w_out.shape)]
    out_shape = [jax.ShapeDtypeStruct(packed[0].shape, BF16)] * nb + [
        jax.ShapeDtypeStruct((ff // lanes, width, lanes), F32),
        jax.ShapeDtypeStruct((ff // lanes, width, lanes), F32),
        jax.ShapeDtypeStruct((2 * nb, rows, lanes), F32),
        jax.ShapeDtypeStruct((2 * nb, max(8, n), lanes), F32),
    ]
    out_specs = [pspec] * nb + [fullo((ff // lanes, width, lanes)), fullo((ff // lanes, width, lanes)), fullo((2 * nb, rows, lanes)), fullo((2 * nb, max(8, n), lanes))]
    args = list(packed) + [prm, w_in, w_out]
    if not first:
        args += list(carried)
        in_specs += [full(v.shape) for v in carried]
    scratch = [
        pltpu.VMEM((nb, length + 2 * PAD, lanes), F32),
        pltpu.VMEM((nb, length + 2 * PAD, lanes), F32),
        pltpu.VMEM((nb, length, lanes), F32),
        pltpu.VMEM((length, width), BF16),
        pltpu.VMEM((length, width), BF16),
        pltpu.VMEM((length, ff), BF16),
        pltpu.VMEM((length, ff), F32),
        pltpu.VMEM((length, ff), BF16),
        pltpu.VMEM((length, width), F32),
        pltpu.VMEM((1, ff), F32),
    ]
    return pl.pallas_call(
        functools.partial(body, nb, taps, speakers, first),
        out_shape=out_shape,
        grid_spec=pltpu.PrefetchScalarGridSpec(
            num_scalar_prefetch=3, grid=(n,), in_specs=in_specs, out_specs=out_specs, scratch_shapes=scratch),
        cost_estimate=pl.CostEstimate(flops=12 * n * length * width * ff, transcendentals=2 * n * length * ff, bytes_accessed=16 * n * length * width),
        compiler_params=pltpu.CompilerParams(dimension_semantics=("arbitrary",), vmem_limit_bytes=50 << 20),
        name="block",
    )(order, spk, live, *args)


def ring(axis, size, shift):
    return lambda v: lax.ppermute(v, axis, [(i, (i + shift) % size) for i in range(size)])


def flip(axis, size, mask):
    return lambda v: lax.ppermute(v, axis, [(i, i ^ mask) for i in range(size)])


def stages(dp_count):
    low, out = 2, []
    while low < dp_count:
        out.append((low, min(4, dp_count // low)))
        low *= 4
    return out


def pick(v, index, axis=0):
    return lax.dynamic_index_in_dim(v, index, axis, keepdims=False)


def spread(pieces, indices, count):
    out = jnp.zeros((count,) + pieces[0].shape, pieces[0].dtype)
    for piece, index in zip(pieces, indices):
        out = lax.dynamic_update_index_in_dim(out, piece, index, 0)
    return out


def gather_dp(v, dp, dp_count):
    for low, count in stages(dp_count):
        here = (dp // low) % count
        v = spread([v] + [flip("dp", dp_count, low * m)(v) for m in range(1, count)],
                   [here] + [here ^ m for m in range(1, count)], count)
        v = v.reshape((-1,) + v.shape[2:]) if v.ndim > 4 else v
    core = dp % 2
    other = flip("dp", dp_count, 1)(v)
    return jnp.where(core == 0, jnp.stack([v, other], 1), jnp.stack([other, v], 1))


def per_device(clips_in, speaker, counts, conv_weight, conv_bias, scale_table, shift_table,
               w_in, b_in, w_out, b_out, layer_scale, grad_out):
    clip_num, length, lanes = clips_in.shape
    nb = lax.axis_size("chan")
    dp_count = lax.axis_size("dp")
    me = lax.axis_index("chan")
    dp = lax.axis_index("dp")
    speakers = scale_table.shape[0]
    taps = conv_weight.shape[0]
    per = w_in.shape[1]
    width, ff = nb * lanes, nb * per
    order = (me - jnp.arange(nb, dtype=jnp.int32)) % nb
    n = clip_num // nb // CHUNKS

    packed = []
    for k in range(CHUNKS):
        part = []
        for d in range(nb):
            at = (k * nb + (me + d) % nb) * n
            block = jnp.stack([lax.dynamic_slice_in_dim(clips_in, at, n), lax.dynamic_slice_in_dim(grad_out, at, n)])
            part.append(ring("chan", nb, d)(block) if d else block)
        packed.append(part)

    rows = [scale_table, shift_table, conv_weight, conv_bias[None], b_out[None], layer_scale[None], b_in.reshape(-1, lanes)]
    prm = jnp.concatenate(rows, 0)
    prm = jnp.pad(prm, ((0, -prm.shape[0] % 16), (0, 0)))
    prm = jnp.stack([prm] + [ring("chan", nb, d)(prm) for d in range(1, nb)]).astype(F32)

    ra, rb = width // dp_count, per // dp_count
    wa = lax.dynamic_slice_in_dim(w_in, dp * ra, ra).reshape(ra, per // lanes, lanes).transpose(1, 0, 2).reshape(-1, lanes)
    wb = lax.dynamic_slice_in_dim(w_out, dp * rb, rb).reshape(rb, nb, lanes).transpose(1, 0, 2).reshape(-1, lanes)
    share = jnp.concatenate([wa, wb])
    share = spread([share] + [ring("chan", nb, d)(share) for d in range(1, nb)],
                   [order[d] for d in range(nb)], nb)
    whole = gather_dp(share, dp, dp_count).reshape(dp_count, nb, -1, lanes)
    split = wa.shape[0]
    w_in_all = whole[:, :, :split].reshape(dp_count, nb, per // lanes, ra, lanes).transpose(0, 3, 1, 2, 4).reshape(width, ff)
    w_out_all = whole[:, :, split:].reshape(dp_count, nb, nb, rb, lanes).transpose(1, 0, 3, 2, 4).reshape(ff, width)

    carried = None
    back = []
    scale_rows, shift_rows, hots = [], [], []
    for k in range(CHUNKS):
        slots = (k * nb + me) * n + jnp.arange(n)
        spk = lax.dynamic_slice_in_dim(speaker, (k * nb + me) * n, n)
        live = (slots < counts[0]).astype(jnp.int32)
        out = block_call(order, spk, live, packed[k], prm, w_in_all, w_out_all, taps, speakers, carried)
        carried = out[nb:nb + 3]
        grow = out[nb + 3]
        hots.append((spk[:, None] == jnp.arange(speakers)[None]).astype(F32))
        scale_rows.append(grow[:nb, :n])
        shift_rows.append(grow[nb:, :n])
        back.append([out[0]] + [ring("chan", nb, -d)(out[d]) for d in range(1, nb)])

    clips_out = jnp.zeros(clips_in.shape, BF16)
    grad_clips = grad_out.astype(F32)
    for k in range(CHUNKS):
        for d in range(nb):
            at = (k * nb + (me + d) % nb) * n
            clips_out = lax.dynamic_update_slice_in_dim(clips_out, back[k][d][0], at, 0)
            g = lax.dynamic_slice_in_dim(grad_out, at, n).astype(F32) + back[k][d][1].astype(F32)
            grad_clips = lax.dynamic_update_slice_in_dim(grad_clips, g, at, 0)

    gwi, gwo, gsm = carried
    hot = jnp.concatenate(hots)
    table = lambda r: jnp.einsum("ns,dnl->dsl", hot, jnp.concatenate(r, 1), precision=lax.Precision.HIGHEST)
    inverse = lambda v: jnp.take(v, order, axis=0)
    small = jnp.concatenate([inverse(table(scale_rows)), inverse(table(shift_rows)), inverse(gsm[:nb]) + gsm[nb:]], 1)
    used = small.shape[1]
    unit = dp_count * 16
    small = jnp.pad(small, ((0, 0), (0, -used % unit), (0, 0)))
    sizes = [gwi.shape[0] // nb * gwi.shape[1], gwo.shape[0] // nb * gwo.shape[1], small.shape[1]]
    parts = [v.reshape(nb, dp_count // 2, 2, -1, lanes) for v in (gwi, gwo, small)]
    core = dp % 2
    mine = jnp.concatenate([pick(v, core, 2) for v in parts], 2)
    other = jnp.concatenate([pick(v, 1 - core, 2) for v in parts], 2).astype(BF16)
    total = mine + flip("dp", dp_count, 1)(other).astype(F32)
    for low, count in reversed(stages(dp_count)):
        here = (dp // low) % count
        v = total.reshape(nb, count, -1, total.shape[-2], lanes)
        total = pick(v, here, 1)
        for m in range(1, count):
            total = total + flip("dp", dp_count, low * m)(pick(v, here ^ m, 1).astype(BF16)).astype(F32)
    v = total.reshape(nb, -1, lanes)
    total = pick(v, me)
    for d in range(1, nb):
        total = total + ring("chan", nb, d)(pick(v, (me + d) % nb).astype(BF16)).astype(F32)
    whole = gather_dp(total.astype(BF16)[None], dp, dp_count).reshape(dp_count, -1, lanes).astype(F32)
    cut = [s // dp_count for s in sizes]
    g_in = whole[:, :cut[0]].reshape(per // lanes, width, lanes).transpose(1, 0, 2).reshape(width, per)
    g_out = whole[:, cut[0]:cut[0] + cut[1]].reshape(per // lanes, width, lanes).transpose(0, 2, 1).reshape(per, width)
    small = whole[:, cut[0] + cut[1]:].reshape(-1, lanes)
    at = 2 * speakers
    return (
        clips_out,
        grad_clips,
        small[at:at + taps],
        small[at + taps],
        small[:speakers],
        small[speakers:at],
        g_in,
        small[at + taps + 3:at + taps + 3 + per // lanes].reshape(per),
        g_out,
        small[at + taps + 1],
        small[at + taps + 2],
    )


def solution(mesh):
    act = P("dp", None, "chan")
    col, vec, row = P(None, "chan"), P("chan"), P("chan", None)
    in_specs = (act, P("dp"), P("dp"), col, vec, col, col, col, vec, row, vec, vec, act)
    out_specs = (act, act, col, vec, col, col, col, vec, row, vec, vec)
    return jax.shard_map(per_device, mesh=mesh, in_specs=in_specs, out_specs=out_specs, check_vma=False)
```

```python
import functools

import jax
import jax.numpy as jnp
from jax import lax
from jax.experimental import pallas as pl
from jax.experimental.pallas import tpu as pltpu
from jax.sharding import PartitionSpec as P

SPLIT = (2, 2)
GROUP = 8

EPS = 1e-06
ROOT_TWO_PI = 2.5066282746310002
F32 = jnp.float32
BF16 = jnp.bfloat16
PAD = 8
HINT = 1 << 36


def gelu_pair(v):
    z = jnp.abs(v)
    t = 1.0 / (1.0 + (0.3275911 * 0.7071067811865476) * z)
    e = jnp.exp(v * v * -0.5)
    poly = t * (0.5 * 0.254829592 + t * (0.5 * -0.284496736 + t * (0.5 * 1.421413741 + t * (0.5 * -1.453152027 + t * (0.5 * 1.061405429)))))
    tail = poly * e
    cdf = jnp.where(v >= 0.0, 1.0 - tail, tail)
    return v * cdf, cdf + v * (e * (1.0 / ROOT_TWO_PI))


def dot(a, b, ca, cb):
    return lax.dot_general(a, b, (((ca,), (cb,)), ((), ())), preferred_element_type=F32)


def body(n_blocks, taps, speakers, small_rows, first, last,
         order_ref, spk_ref, live_ref, meta_ref, *refs):
    nb = n_blocks
    x0, g0 = refs[:2]
    p = refs[2:nb + 1]
    prm, w_in, w_out = refs[nb + 1:nb + 4]
    k = nb + 4
    if not first:
        got = refs[k:k + 3]
        k += 3
    o = refs[k:k + nb]
    k += nb
    if last:
        keep, send = refs[k:k + 2]
        gwi, gwo, gsm = refs[-3:]
        k += 2
    else:
        gwi, gwo, gsm = refs[k:k + 3]
        k += 3
    (xpad, gpad, normed, nlow, blow, act, slope, plow, wide, b_in) = refs[k:k + 10]
    i = pl.program_id(0)
    length, lanes = normed.shape[1], normed.shape[2]
    width = nb * lanes
    ff = act.shape[1]
    per = ff // nb
    tiles = per // lanes
    margin = taps // 2
    r_conv, r_cb = 2 * speakers, 2 * speakers + taps
    r_bo, r_ls, r_bi = r_cb + 1, r_cb + 2, r_cb + 3
    cols = [pl.multiple_of(order_ref[d] * lanes, lanes) for d in range(nb)]
    xs = [x0] + [q.at[0] for q in p]
    gs = [g0] + [q.at[1] for q in p]

    @pl.when(i == 0)
    def _():
        for d in range(nb):
            zero = jnp.zeros((PAD, lanes), F32)
            xpad[d, 0:PAD, :] = zero
            xpad[d, PAD + length:, :] = zero
            gpad[d, 0:PAD, :] = zero
            gpad[d, PAD + length:, :] = zero
            for r in range(tiles):
                at = pl.multiple_of(order_ref[d] * per + r * lanes, lanes)
                b_in[:, pl.ds(at, lanes)] = prm[d, r_bi + r:r_bi + r + 1, :]
        if first:
            gwi[...] = jnp.zeros_like(gwi)
            gwo[...] = jnp.zeros_like(gwo)
            gsm[...] = jnp.zeros_like(gsm)
        else:
            gwi[...] = got[0][...]
            gwo[...] = got[1][...]
            gsm[...] = got[2][...]

    spk = spk_ref[i]
    live = live_ref[i].astype(F32)
    total = jnp.zeros((length, 1), F32)
    for d in range(nb):
        xpad[d, PAD:PAD + length, :] = xs[d][0].astype(F32)
        acc = jnp.broadcast_to(prm[d, r_cb:r_cb + 1, :], (length, lanes))
        for t in range(taps):
            s = PAD - margin + t
            acc = acc + prm[d, r_conv + t:r_conv + t + 1, :] * xpad[d, s:s + length, :]
        normed[d] = acc
        total = total + jnp.sum(acc, 1, keepdims=True)
    mean = total / width
    square = jnp.zeros((length, 1), F32)
    for d in range(nb):
        c = normed[d] - mean
        normed[d] = c
        square = square + jnp.sum(c * c, 1, keepdims=True)
    inv = lax.rsqrt(square / width + EPS)
    for d in range(nb):
        v = normed[d] * inv
        normed[d] = v
        sc = prm[d, pl.ds(spk, 1), :]
        sh = prm[d, pl.ds(speakers + spk, 1), :]
        nlow[:, pl.ds(cols[d], lanes)] = (v * sc + sh).astype(BF16)

    step = 256
    for f in range(0, ff, step):
        pre = dot(nlow[...], w_in[:, f:f + step], 1, 0) + b_in[:, f:f + step]
        a, s = gelu_pair(pre)
        act[:, f:f + step] = a.astype(BF16)
        slope[:, f:f + step] = s
    wide[...] = dot(act[...], w_out[...], 1, 0)
    for d in range(nb):
        b = wide[:, pl.ds(cols[d], lanes)] + prm[d, r_bo:r_bo + 1, :]
        ls = prm[d, r_ls:r_ls + 1, :] * live
        x = xs[d][0].astype(F32)
        g = gs[d][0].astype(F32)
        o[d][0, 0] = (x + b * ls).astype(BF16)
        gb = g * ls
        gsm[d, r_bo:r_bo + 1, :] += jnp.sum(gb, 0, keepdims=True)
        gsm[d, r_ls:r_ls + 1, :] += jnp.sum(g * b, 0, keepdims=True) * live
        blow[:, pl.ds(cols[d], lanes)] = gb.astype(BF16)
    for f in range(0, ff, step):
        gp = dot(blow[...], w_out[f:f + step, :], 1, 1) * slope[:, f:f + step]
        low = gp.astype(BF16)
        plow[:, f:f + step] = low
        at = f // lanes
        gsum = jnp.sum(gp, 0, keepdims=True)
        for r in range(step // lanes):
            q = at + r
            gsm[nb, q:q + 1, :] += gsum[:, r * lanes:(r + 1) * lanes]
        da = dot(nlow[...], low, 0, 0)
        for r in range(step // lanes):
            gwi[at + r] += da[:, r * lanes:(r + 1) * lanes]
        gwo[f:f + step, :] += dot(act[:, f:f + step], blow[...], 0, 0)
    wide[...] = dot(plow[...], w_in[...], 1, 1)
    m1 = jnp.zeros((length, 1), F32)
    m2 = jnp.zeros((length, 1), F32)
    for d in range(nb):
        gn = wide[:, pl.ds(cols[d], lanes)]
        v = normed[d]
        gv = gn * v
        gsm[d, pl.ds(spk, 1), :] += jnp.sum(gv, 0, keepdims=True)
        gsm[d, pl.ds(speakers + spk, 1), :] += jnp.sum(gn, 0, keepdims=True)
        sc = prm[d, pl.ds(spk, 1), :]
        m1 = m1 + jnp.sum(gn * sc, 1, keepdims=True)
        m2 = m2 + jnp.sum(gv * sc, 1, keepdims=True)
    m1 = m1 / width
    m2 = m2 / width
    for d in range(nb):
        sc = prm[d, pl.ds(spk, 1), :]
        gc = (wide[:, pl.ds(cols[d], lanes)] * sc - m1 - normed[d] * m2) * inv
        gpad[d, PAD:PAD + length, :] = gc
        gsm[d, r_cb:r_cb + 1, :] += jnp.sum(gc, 0, keepdims=True)
        acc = jnp.zeros((length, lanes), F32)
        for t in range(taps):
            s = PAD - margin + t
            gsm[d, r_conv + t:r_conv + t + 1, :] += jnp.sum(xpad[d, s:s + length, :] * gc, 0, keepdims=True)
            s = PAD + margin - t
            acc = acc + prm[d, r_conv + t:r_conv + t + 1, :] * gpad[d, s:s + length, :]
        o[d][1, 0] = acc.astype(BF16)

    if last:
        @pl.when(i == pl.num_programs(0) - 1)
        def _():
            place = meta_ref[1]
            ra, rb, rs = width // GROUP, per // GROUP, small_rows // GROUP
            for d in range(nb):
                c = order_ref[d]
                for r in range(tiles):
                    gsm[d, r_bi + r:r_bi + r + 1, :] = gsm[nb, pl.ds(c * tiles + r, 1), :]

            def emit(m, carry):
                for e in range(nb):
                    d = -e % nb
                    c = order_ref[d]
                    for out, part in ((keep, place ^ (2 * m)), (send, place ^ (2 * m) ^ 1)):
                        for r in range(tiles):
                            v = gwi[c * tiles + r, pl.ds(pl.multiple_of(part * ra, ra), ra), :]
                            out[m, e, r * ra:(r + 1) * ra, :] = v.astype(out.dtype)
                        base = tiles * ra
                        for r in range(nb):
                            v = gwo[pl.ds(pl.multiple_of(c * per + part * rb, 16), rb), r * lanes:(r + 1) * lanes]
                            out[m, e, base + r * rb:base + (r + 1) * rb, :] = v.astype(out.dtype)
                        base += nb * rb
                        v = gsm[d, pl.ds(pl.multiple_of(part * rs, rs), rs), :]
                        out[m, e, base:base + rs, :] = v.astype(out.dtype)
                return carry
            lax.fori_loop(0, GROUP // 2, emit, 0)


def block_call(order, spk, live, meta, clips, grads, packed, prm, w_in, w_out, taps, speakers, small_rows, carried, last):
    nb = len(packed) + 1
    _, n, length, lanes = packed[0].shape
    width = nb * lanes
    ff = w_in.shape[1]
    per = ff // nb
    first = carried is None
    full = lambda shape: pl.BlockSpec(shape, lambda i, *_: (0,) * len(shape), pipeline_mode=pl.Buffered(1))
    fullo = lambda shape: pl.BlockSpec(shape, lambda i, *_: (0,) * len(shape))
    pspec = pl.BlockSpec((2, 1, length, lanes), lambda i, *_: (0, i, 0, 0))
    own = pl.BlockSpec((1, length, lanes), lambda i, order, spk, live, meta: (meta[0] + i, 0, 0))
    in_specs = [own, own] + [pspec] * (nb - 1) + [full(prm.shape), full(w_in.shape), full(w_out.shape)]
    sums = [(ff // lanes, width, lanes), (ff, width), (nb + 1, small_rows, lanes)]
    rows = (width // GROUP) * (per // lanes) + (per // GROUP) * nb + small_rows // GROUP
    out_shape = [jax.ShapeDtypeStruct(packed[0].shape, BF16)] * nb
    out_specs = [pspec] * nb
    if last:
        out_shape += [jax.ShapeDtypeStruct((GROUP // 2, nb, rows, lanes), t) for t in (F32, BF16)]
        out_specs += [fullo((GROUP // 2, nb, rows, lanes))] * 2
    else:
        out_shape += [jax.ShapeDtypeStruct(s, F32) for s in sums]
        out_specs += [fullo(s) for s in sums]
    args = [clips, grads] + list(packed) + [prm, w_in, w_out]
    if not first:
        args += list(carried)
        in_specs += [full(v.shape) for v in carried]
    scratch = [
        pltpu.VMEM((nb, length + 2 * PAD, lanes), F32),
        pltpu.VMEM((nb, length + 2 * PAD, lanes), F32),
        pltpu.VMEM((nb, length, lanes), F32),
        pltpu.VMEM((length, width), BF16),
        pltpu.VMEM((length, width), BF16),
        pltpu.VMEM((length, ff), BF16),
        pltpu.VMEM((length, ff), F32),
        pltpu.VMEM((length, ff), BF16),
        pltpu.VMEM((length, width), F32),
        pltpu.VMEM((1, ff), F32),
    ]
    if last:
        scratch += [pltpu.VMEM(s, F32) for s in sums]
    return pl.pallas_call(
        functools.partial(body, nb, taps, speakers, small_rows, first, last),
        out_shape=out_shape,
        grid_spec=pltpu.PrefetchScalarGridSpec(
            num_scalar_prefetch=4, grid=(n,), in_specs=in_specs, out_specs=out_specs, scratch_shapes=scratch),
        cost_estimate=pl.CostEstimate(flops=(HINT if last else 0), transcendentals=0, bytes_accessed=0),
        compiler_params=pltpu.CompilerParams(dimension_semantics=("arbitrary",), vmem_limit_bytes=56 << 20),
        name="block",
    )(order, spk, live, meta, *args)


def stack_body(count, rows, *refs):
    ins, (w, prm) = refs[:count], refs[count:]
    for d in range(count):
        w[d] = ins[d][0:rows, :]
        prm[d] = ins[d][rows:, :].astype(F32)


def stack_call(parts, rows, hint):
    total, lanes = parts[0].shape
    return pl.pallas_call(
        functools.partial(stack_body, len(parts), rows),
        out_shape=[jax.ShapeDtypeStruct((len(parts), rows, lanes), BF16),
                   jax.ShapeDtypeStruct((len(parts), total - rows, lanes), F32)],
        cost_estimate=pl.CostEstimate(flops=hint, transcendentals=0, bytes_accessed=0),
        name="gathered",
    )(*parts)


def whole_body(nb, ra, rb, tiles, lanes, order_ref, meta_ref, *refs):
    ins, (w_in, w_out) = [refs[s % 2].at[s // 2] for s in range(GROUP)], refs[2:]
    per = tiles * lanes
    for s in range(GROUP):
        part = meta_ref[1] ^ s

        def go(d, carry):
            c = order_ref[d]
            for r in range(tiles):
                w_in[pl.ds(pl.multiple_of(part * ra, ra), ra), pl.ds(pl.multiple_of(c * per + r * lanes, lanes), lanes)] = ins[s][d, r * ra:(r + 1) * ra, :]
            base = tiles * ra
            for r in range(nb):
                w_out[pl.ds(pl.multiple_of(c * per + part * rb, 16), rb), r * lanes:(r + 1) * lanes] = ins[s][d, base + r * rb:base + (r + 1) * rb, :]
            return carry
        lax.fori_loop(0, nb, go, 0)


def whole_call(order, meta, parts, ra, rb, tiles):
    _, nb, rows, lanes = parts[0].shape
    width, ff = nb * lanes, nb * tiles * lanes
    vm = pl.BlockSpec(memory_space=pltpu.VMEM)
    sm = pl.BlockSpec(memory_space=pltpu.SMEM)
    return pl.pallas_call(
        functools.partial(whole_body, nb, ra, rb, tiles, lanes),
        in_specs=[sm, sm] + [vm] * 2,
        out_specs=[vm, vm],
        out_shape=[jax.ShapeDtypeStruct((width, ff), BF16), jax.ShapeDtypeStruct((ff, width), BF16)],
        name="weights",
    )(order, meta, *parts)


def finish_body(nb, ra, rb, rs, tiles, lanes, taps, speakers, meta_ref, *refs):
    ins = [refs[s % 2].at[s // 2] for s in range(GROUP)]
    g_in, g_out, scale, shift, conv, cb, bo, ls, bi, small = refs[2:]
    for s in range(GROUP):
        part = meta_ref[1] ^ s
        for r in range(tiles):
            g_in[pl.ds(pl.multiple_of(part * ra, ra), ra), r * lanes:(r + 1) * lanes] = ins[s][r * ra:(r + 1) * ra, :].astype(F32)
        base = tiles * ra
        for r in range(nb):
            g_out[pl.ds(pl.multiple_of(part * rb, 16), rb), r * lanes:(r + 1) * lanes] = ins[s][base + r * rb:base + (r + 1) * rb, :].astype(F32)
        base += nb * rb
        small[pl.ds(pl.multiple_of(part * rs, rs), rs), :] = ins[s][base:base + rs, :].astype(F32)
    scale[...] = small[0:speakers, :]
    shift[...] = small[speakers:2 * speakers, :]
    at = 2 * speakers
    conv[...] = small[at:at + taps, :]
    at += taps
    cb[...] = small[at:at + 1, :]
    bo[...] = small[at + 1:at + 2, :]
    ls[...] = small[at + 2:at + 3, :]
    for r in range(tiles):
        bi[:, r * lanes:(r + 1) * lanes] = small[at + 3 + r:at + 4 + r, :]


def finish_call(meta, parts, nb, ra, rb, rs, tiles, taps, speakers):
    lanes = parts[0].shape[2]
    vm = pl.BlockSpec(memory_space=pltpu.VMEM)
    sm = pl.BlockSpec(memory_space=pltpu.SMEM)
    shapes = [(nb * lanes, tiles * lanes), (tiles * lanes, nb * lanes), (speakers, lanes), (speakers, lanes), (taps, lanes),
              (1, lanes), (1, lanes), (1, lanes), (1, tiles * lanes)]
    return pl.pallas_call(
        functools.partial(finish_body, nb, ra, rb, rs, tiles, lanes, taps, speakers),
        in_specs=[sm] + [vm] * 2,
        out_specs=[vm] * len(shapes),
        out_shape=[jax.ShapeDtypeStruct(s, F32) for s in shapes],
        scratch_shapes=[pltpu.VMEM((rs * GROUP, lanes), F32)],
        name="finish",
    )(meta, *parts)


def ring(axis, size, shift):
    return lambda v: lax.ppermute(v, axis, [(i, (i + shift) % size) for i in range(size)])


def flip(axis, size, mask):
    return lambda v: lax.ppermute(v, axis, [(i, i ^ mask) for i in range(size)])


def gather_group(v, dp_count, after=()):
    a, b = flip("dp", dp_count, 2)(v), flip("dp", dp_count, 4)(v)
    near = jnp.stack([v, a, b, flip("dp", dp_count, 4)(a)])
    near, *after = lax.optimization_barrier((near, *after))
    return [near, flip("dp", dp_count, 1)(near)], after


def per_device(clips_in, speaker, counts, conv_weight, conv_bias, scale_table, shift_table,
               w_in, b_in, w_out, b_out, layer_scale, grad_out):
    clip_num, length, lanes = clips_in.shape
    nb = lax.axis_size("chan")
    dp_count = lax.axis_size("dp")
    me = lax.axis_index("chan")
    dp = lax.axis_index("dp")
    speakers = scale_table.shape[0]
    taps = conv_weight.shape[0]
    per = w_in.shape[1]
    tiles = per // lanes
    width = nb * lanes
    order = (me - jnp.arange(nb, dtype=jnp.int32)) % nb
    place = dp % GROUP
    slots = clip_num // nb
    sizes = [slots * c // sum(SPLIT) for c in SPLIT]
    starts = [nb * sum(sizes[:k]) for k in range(len(sizes))]

    ra, rb = width // GROUP, per // GROUP
    wa = lax.dynamic_slice_in_dim(w_in, place * ra, ra).reshape(ra, tiles, lanes).transpose(1, 0, 2).reshape(-1, lanes)
    wb = lax.dynamic_slice_in_dim(w_out, place * rb, rb).reshape(rb, nb, lanes).transpose(1, 0, 2).reshape(-1, lanes)
    rows = [wa, wb, scale_table, shift_table, conv_weight, conv_bias[None], b_out[None], layer_scale[None], b_in.reshape(-1, lanes)]
    used = sum(r.shape[0] for r in rows[2:])
    small_rows = -(-used // (GROUP * 16)) * GROUP * 16
    share = jnp.pad(jnp.concatenate(rows), ((0, -used % 16), (0, 0)))
    shares = [share] + [ring("chan", nb, d)(share) for d in range(1, nb)]

    packed = []
    for k, n in enumerate(sizes):
        part = []
        for d in range(1, nb):
            at = starts[k] + (me + d) % nb * n
            block = jnp.stack([lax.dynamic_slice_in_dim(clips_in, at, n), lax.dynamic_slice_in_dim(grad_out, at, n)])
            part.append(ring("chan", nb, d)(block))
        packed.append(part)

    stacked, prm = stack_call(shares, wa.shape[0] + wb.shape[0], 0)
    meta = jnp.stack([me, place]).astype(jnp.int32)
    gathered, packed[0] = gather_group(stacked, dp_count, packed[0])
    w_in_all, w_out_all = whole_call(order, meta, gathered, ra, rb, tiles)

    carried = None
    back = []
    for k, n in enumerate(sizes):
        base = starts[k] + me * n
        spk = lax.dynamic_slice_in_dim(speaker, base, n)
        live = (base + jnp.arange(n) < counts[0]).astype(jnp.int32)
        last = k == len(sizes) - 1
        out = block_call(order, spk, live, jnp.stack([base, place]).astype(jnp.int32), clips_in, grad_out, packed[k],
                         prm, w_in_all, w_out_all, taps, speakers, small_rows, carried, last)
        carried = out[nb:]
        back.append([out[0]] + [ring("chan", nb, -d)(out[d]) for d in range(1, nb)])

    keep, send = carried
    send, *back[0] = lax.optimization_barrier((send, *back[0]))
    got = flip("dp", dp_count, 1)(send)
    total = keep[0] + got[0].astype(F32)
    for m in range(1, GROUP // 2):
        total = total + flip("dp", dp_count, 2 * m)((keep[m] + got[m].astype(F32)).astype(BF16)).astype(F32)
    step = GROUP
    while step < dp_count:
        low = total.astype(BF16)
        total = low.astype(F32) + flip("dp", dp_count, step)(low).astype(F32)
        step *= 2
    mine = total[0]
    for d in range(1, nb):
        mine = mine + ring("chan", nb, d)(total[d].astype(BF16)).astype(F32)
    g_in, g_out, g_scale, g_shift, g_conv, g_cb, g_bo, g_ls, g_bi = finish_call(
        meta, gather_group(mine.astype(BF16), dp_count)[0], nb, ra, rb, small_rows // GROUP, tiles, taps, speakers)

    clips_out = jnp.zeros(clips_in.shape, BF16)
    grad_clips = grad_out.astype(F32)
    for k, n in enumerate(sizes):
        for d in range(nb):
            at = starts[k] + (me + d) % nb * n
            clips_out = lax.dynamic_update_slice_in_dim(clips_out, back[k][d][0], at, 0)
            g = lax.dynamic_slice_in_dim(grad_out, at, n).astype(F32) + back[k][d][1].astype(F32)
            grad_clips = lax.dynamic_update_slice_in_dim(grad_clips, g, at, 0)

    return (clips_out, grad_clips, g_conv, g_cb.reshape(lanes), g_scale, g_shift, g_in, g_bi.reshape(per), g_out,
            g_bo.reshape(lanes), g_ls.reshape(lanes))


def solution(mesh):
    act = P("dp", None, "chan")
    col, vec, row = P(None, "chan"), P("chan"), P("chan", None)
    in_specs = (act, P("dp"), P("dp"), col, vec, col, col, col, vec, row, vec, vec, act)
    out_specs = (act, act, col, vec, col, col, col, vec, row, vec, vec)
    return jax.shard_map(per_device, mesh=mesh, in_specs=in_specs, out_specs=out_specs, check_vma=False)
```

```python
import functools

import jax
import jax.numpy as jnp
from jax import lax
from jax.experimental import pallas as pl
from jax.experimental.pallas import tpu as pltpu
from jax.sharding import PartitionSpec as P

RUNS = ((1, 1), (2,))
GROUP = 8

EPS = 1e-06
ROOT_TWO_PI = 2.5066282746310002
F32 = jnp.float32
BF16 = jnp.bfloat16
PAD = 8
HINT = 1 << 36


def gelu_pair(v):
    z = jnp.abs(v)
    t = 1.0 / (1.0 + (0.3275911 * 0.7071067811865476) * z)
    e = jnp.exp(v * v * -0.5)
    poly = t * (0.5 * 0.254829592 + t * (0.5 * -0.284496736 + t * (0.5 * 1.421413741 + t * (0.5 * -1.453152027 + t * (0.5 * 1.061405429)))))
    tail = poly * e
    cdf = jnp.where(v >= 0.0, 1.0 - tail, tail)
    return v * cdf, cdf + v * (e * (1.0 / ROOT_TWO_PI))


def dot(a, b, ca, cb):
    return lax.dot_general(a, b, (((ca,), (cb,)), ((), ())), preferred_element_type=F32)


def body(n_blocks, taps, speakers, runs, first,
         order_ref, spk_ref, live_ref, slot_ref, meta_ref, *refs):
    nb = n_blocks
    x0, g0 = refs[:2]
    k = 2
    p = []
    for _ in runs:
        p.append(refs[k:k + nb - 1])
        k += nb - 1
    prm = refs[k]
    shares = refs[k + 1:k + 1 + GROUP]
    k += 1 + GROUP
    if not first:
        got = refs[k]
        k += 1
    o = refs[k:k + nb]
    k += nb
    (nlow, blow, act, plow, gsm, xpad, gpad, normed, gin, slope, wide, b_in, w_in, w_out) = refs[k:k + 14]
    i = pl.program_id(0)
    length, lanes = normed.shape[1], normed.shape[2]
    width = nb * lanes
    ff = act.shape[2]
    per = ff // nb
    tiles = per // lanes
    margin = taps // 2
    r_conv, r_cb = 2 * speakers, 2 * speakers + taps
    r_bo, r_ls, r_bi = r_cb + 1, r_cb + 2, r_cb + 3
    cols = [pl.multiple_of(order_ref[d] * lanes, lanes) for d in range(nb)]

    @pl.when(i == 0)
    def _():
        for d in range(nb):
            zero = jnp.zeros((PAD, lanes), F32)
            xpad[d, 0:PAD, :] = zero
            xpad[d, PAD + length:, :] = zero
            gpad[d, 0:PAD, :] = zero
            gpad[d, PAD + length:, :] = zero
            for r in range(tiles):
                at = pl.multiple_of(order_ref[d] * per + r * lanes, lanes)
                b_in[:, pl.ds(at, lanes)] = prm[d, r_bi + r:r_bi + r + 1, :]
        gsm[...] = jnp.zeros_like(gsm) if first else got[...]
        ra, rb = width // GROUP, per // GROUP
        for s in range(GROUP):
            part = meta_ref[1] ^ s

            def unpack(d, carry):
                c = order_ref[d]
                for r in range(tiles):
                    w_in[pl.ds(pl.multiple_of(part * ra, ra), ra), pl.ds(pl.multiple_of(c * per + r * lanes, lanes), lanes)] = shares[s][d, r * ra:(r + 1) * ra, :]
                base = tiles * ra
                for r in range(nb):
                    w_out[pl.ds(pl.multiple_of(c * per + part * rb, 16), rb), r * lanes:(r + 1) * lanes] = shares[s][d, base + r * rb:base + (r + 1) * rb, :]
                return carry
            lax.fori_loop(0, nb, unpack, 0)

    xpad[0, PAD:PAD + length, :] = x0[0].astype(F32)
    gin[0] = g0[0]
    low = 0
    for run, part in zip(runs, p):
        @pl.when((i >= low) & (i < low + run))
        def _(low=low, run=run, part=part):
            at = i - low if run > 1 else 0
            for d in range(1, nb):
                xpad[d, PAD:PAD + length, :] = part[d - 1][0, at].astype(F32)
                gin[d] = part[d - 1][1, at]
        low += run

    spk = spk_ref[i]
    live = live_ref[i].astype(F32)
    total = jnp.zeros((length, 1), F32)
    for d in range(nb):
        acc = jnp.broadcast_to(prm[d, r_cb:r_cb + 1, :], (length, lanes))
        for t in range(taps):
            s = PAD - margin + t
            acc = acc + prm[d, r_conv + t:r_conv + t + 1, :] * xpad[d, s:s + length, :]
        normed[d] = acc
        total = total + jnp.sum(acc, 1, keepdims=True)
    mean = total / width
    square = jnp.zeros((length, 1), F32)
    for d in range(nb):
        c = normed[d] - mean
        normed[d] = c
        square = square + jnp.sum(c * c, 1, keepdims=True)
    inv = lax.rsqrt(square / width + EPS)
    for d in range(nb):
        v = normed[d] * inv
        normed[d] = v
        sc = prm[d, pl.ds(spk, 1), :]
        sh = prm[d, pl.ds(speakers + spk, 1), :]
        nlow[0, :, pl.ds(cols[d], lanes)] = (v * sc + sh).astype(BF16)

    step = 256
    for f in range(0, ff, step):
        pre = dot(nlow[0], w_in[:, f:f + step], 1, 0) + b_in[:, f:f + step]
        a, s = gelu_pair(pre)
        act[0, :, f:f + step] = a.astype(BF16)
        slope[:, f:f + step] = s
    wide[...] = dot(act[0], w_out[...], 1, 0)
    for d in range(nb):
        b = wide[:, pl.ds(cols[d], lanes)] + prm[d, r_bo:r_bo + 1, :]
        ls = prm[d, r_ls:r_ls + 1, :] * live
        x = xpad[d, PAD:PAD + length, :]
        g = gin[d].astype(F32)
        o[d][0, 0] = (x + b * ls).astype(BF16)
        gb = g * ls
        gsm[d, r_bo:r_bo + 1, :] += jnp.sum(gb, 0, keepdims=True)
        gsm[d, r_ls:r_ls + 1, :] += jnp.sum(g * b, 0, keepdims=True) * live
        blow[0, :, pl.ds(cols[d], lanes)] = gb.astype(BF16)
    for f in range(0, ff, step):
        gp = dot(blow[0], w_out[f:f + step, :], 1, 1) * slope[:, f:f + step]
        plow[0, :, f:f + step] = gp.astype(BF16)
        gsum = jnp.sum(gp, 0, keepdims=True)
        for r in range(step // lanes):
            q = f // lanes + r
            gsm[nb, q:q + 1, :] += gsum[:, r * lanes:(r + 1) * lanes]
    wide[...] = dot(plow[0], w_in[...], 1, 1)
    m1 = jnp.zeros((length, 1), F32)
    m2 = jnp.zeros((length, 1), F32)
    for d in range(nb):
        gn = wide[:, pl.ds(cols[d], lanes)]
        v = normed[d]
        gv = gn * v
        gsm[d, pl.ds(spk, 1), :] += jnp.sum(gv, 0, keepdims=True)
        gsm[d, pl.ds(speakers + spk, 1), :] += jnp.sum(gn, 0, keepdims=True)
        sc = prm[d, pl.ds(spk, 1), :]
        m1 = m1 + jnp.sum(gn * sc, 1, keepdims=True)
        m2 = m2 + jnp.sum(gv * sc, 1, keepdims=True)
    m1 = m1 / width
    m2 = m2 / width
    for d in range(nb):
        sc = prm[d, pl.ds(spk, 1), :]
        gc = (wide[:, pl.ds(cols[d], lanes)] * sc - m1 - normed[d] * m2) * inv
        gpad[d, PAD:PAD + length, :] = gc
        gsm[d, r_cb:r_cb + 1, :] += jnp.sum(gc, 0, keepdims=True)
        acc = jnp.zeros((length, lanes), F32)
        for t in range(taps):
            s = PAD - margin + t
            gsm[d, r_conv + t:r_conv + t + 1, :] += jnp.sum(xpad[d, s:s + length, :] * gc, 0, keepdims=True)
            s = PAD + margin - t
            acc = acc + prm[d, r_conv + t:r_conv + t + 1, :] * gpad[d, s:s + length, :]
        o[d][1, 0] = acc.astype(BF16)


def block_call(order, spk, live, slot, meta, clips, grads, packed, prm, shares, ff, taps, speakers, small_rows, carried, hint):
    nb = len(packed[0]) + 1
    runs = [part[0].shape[1] for part in packed]
    n = sum(runs)
    _, _, length, lanes = packed[0][0].shape
    width = nb * lanes
    first = carried is None
    full = lambda shape: pl.BlockSpec(shape, lambda i, *_: (0,) * len(shape), pipeline_mode=pl.Buffered(1))
    step = lambda *shape: pl.BlockSpec((1,) + shape, lambda i, *_: (i,) + (0,) * len(shape))
    own = pl.BlockSpec((1, length, lanes), lambda i, order, spk, live, slot, meta: (slot[i], 0, 0))
    sums = (nb + 1, small_rows, lanes)
    args = [clips, grads] + [v for part in packed for v in part] + [prm] + list(shares)
    in_specs = [own, own] + [full(v.shape) for v in args[2:]]
    out_shape = [jax.ShapeDtypeStruct((2, n, length, lanes), BF16)] * nb + [
        jax.ShapeDtypeStruct((n, length, w), BF16) for w in (width, width, ff, ff)] + [jax.ShapeDtypeStruct(sums, F32)]
    out_specs = [pl.BlockSpec((2, 1, length, lanes), lambda i, *_: (0, i, 0, 0))] * nb + [step(length, w) for w in (width, width, ff, ff)] + [
        pl.BlockSpec(sums, lambda i, *_: (0, 0, 0))]
    if not first:
        args.append(carried)
        in_specs.append(full(sums))
    scratch = [
        pltpu.VMEM((nb, length + 2 * PAD, lanes), F32),
        pltpu.VMEM((nb, length + 2 * PAD, lanes), F32),
        pltpu.VMEM((nb, length, lanes), F32),
        pltpu.VMEM((nb, length, lanes), BF16),
        pltpu.VMEM((length, ff), F32),
        pltpu.VMEM((length, width), F32),
        pltpu.VMEM((1, ff), F32),
        pltpu.VMEM((width, ff), BF16),
        pltpu.VMEM((ff, width), BF16),
    ]
    return pl.pallas_call(
        functools.partial(body, nb, taps, speakers, runs, first),
        out_shape=out_shape,
        grid_spec=pltpu.PrefetchScalarGridSpec(
            num_scalar_prefetch=5, grid=(n,), in_specs=in_specs, out_specs=out_specs, scratch_shapes=scratch),
        cost_estimate=pl.CostEstimate(flops=hint, transcendentals=0, bytes_accessed=0),
        compiler_params=pltpu.CompilerParams(dimension_semantics=("arbitrary",), vmem_limit_bytes=40 << 20),
        name="block",
    )(order, spk, live, slot, meta, *args)


def grads_body(nb, count, bi_row, order_ref, meta_ref, *refs):
    nlow, blow, act, plow = (refs[j * count:(j + 1) * count] for j in range(4))
    sums, keep, send, gwi, gwo, gsm = refs[4 * count:]
    tiles_all, width, lanes = gwi.shape
    ff = gwo.shape[0]
    tiles = tiles_all // nb
    per = ff // nb
    step = 256
    for f in range(0, ff, step):
        da = sum(dot(a[...], v[:, f:f + step], 0, 0) for a, v in zip(nlow, plow))
        for r in range(step // lanes):
            gwi[f // lanes + r] = da[:, r * lanes:(r + 1) * lanes]
        gwo[f:f + step, :] = sum(dot(v[:, f:f + step], b[...], 0, 0) for v, b in zip(act, blow))
    gsm[...] = sums[0:nb]
    for d in range(nb):
        for r in range(tiles):
            gsm[d, bi_row + r:bi_row + r + 1, :] = sums[nb, pl.ds(order_ref[d] * tiles + r, 1), :]
    place = meta_ref[1]
    ra, rb, rs = width // GROUP, per // GROUP, gsm.shape[1] // GROUP

    def emit(m, carry):
        for e in range(nb):
            d = -e % nb
            c = order_ref[d]
            for out, part in ((keep, place ^ (2 * m)), (send, place ^ (2 * m) ^ 1)):
                for r in range(tiles):
                    v = gwi[c * tiles + r, pl.ds(pl.multiple_of(part * ra, ra), ra), :]
                    out[m, e, r * ra:(r + 1) * ra, :] = v.astype(out.dtype)
                base = tiles * ra
                for r in range(nb):
                    v = gwo[pl.ds(pl.multiple_of(c * per + part * rb, 16), rb), r * lanes:(r + 1) * lanes]
                    out[m, e, base + r * rb:base + (r + 1) * rb, :] = v.astype(out.dtype)
                base += nb * rb
                v = gsm[d, pl.ds(pl.multiple_of(part * rs, rs), rs), :]
                out[m, e, base:base + rs, :] = v.astype(out.dtype)
        return carry
    lax.fori_loop(0, GROUP // 2, emit, 0)


def grads_call(order, meta, nlow, blow, act, plow, sums, bi_row):
    nb = sums.shape[0] - 1
    small_rows, lanes = sums.shape[1:]
    ff = act[0].shape[-1]
    width = nb * lanes
    per = ff // nb
    rows = (width // GROUP) * (per // lanes) + (per // GROUP) * nb + small_rows // GROUP
    flat = [v.reshape(-1, v.shape[-1]) for v in (*nlow, *blow, *act, *plow)]
    vm = pl.BlockSpec(memory_space=pltpu.VMEM)
    sm = pl.BlockSpec(memory_space=pltpu.SMEM)
    return pl.pallas_call(
        functools.partial(grads_body, nb, len(nlow), bi_row),
        in_specs=[sm, sm] + [vm] * (len(flat) + 1),
        out_specs=[vm, vm],
        out_shape=[jax.ShapeDtypeStruct((GROUP // 2, nb, rows, lanes), t) for t in (F32, BF16)],
        scratch_shapes=[pltpu.VMEM((ff // lanes, width, lanes), F32), pltpu.VMEM((ff, width), F32), pltpu.VMEM((nb, small_rows, lanes), F32)],
        cost_estimate=pl.CostEstimate(flops=HINT, transcendentals=0, bytes_accessed=0),
        compiler_params=pltpu.CompilerParams(vmem_limit_bytes=40 << 20),
        name="weight_grads",
    )(order, meta, *flat, sums)


def stack_body(count, rows, *refs):
    ins, (w, prm) = refs[:count], refs[count:]
    for d in range(count):
        w[d] = ins[d][0:rows, :]
        prm[d] = ins[d][rows:, :].astype(F32)


def stack_call(parts, rows, hint):
    total, lanes = parts[0].shape
    return pl.pallas_call(
        functools.partial(stack_body, len(parts), rows),
        out_shape=[jax.ShapeDtypeStruct((len(parts), rows, lanes), BF16),
                   jax.ShapeDtypeStruct((len(parts), total - rows, lanes), F32)],
        cost_estimate=pl.CostEstimate(flops=hint, transcendentals=0, bytes_accessed=0),
        name="gathered",
    )(*parts)


def finish_body(nb, ra, rb, rs, tiles, lanes, taps, speakers, meta_ref, *refs):
    ins = [refs[s % 2].at[s // 2] for s in range(GROUP)]
    g_in, g_out, scale, shift, conv, cb, bo, ls, bi, small = refs[2:]
    for s in range(GROUP):
        part = meta_ref[1] ^ s
        for r in range(tiles):
            g_in[pl.ds(pl.multiple_of(part * ra, ra), ra), r * lanes:(r + 1) * lanes] = ins[s][r * ra:(r + 1) * ra, :].astype(F32)
        base = tiles * ra
        for r in range(nb):
            g_out[pl.ds(pl.multiple_of(part * rb, 16), rb), r * lanes:(r + 1) * lanes] = ins[s][base + r * rb:base + (r + 1) * rb, :].astype(F32)
        base += nb * rb
        small[pl.ds(pl.multiple_of(part * rs, rs), rs), :] = ins[s][base:base + rs, :].astype(F32)
    scale[...] = small[0:speakers, :]
    shift[...] = small[speakers:2 * speakers, :]
    at = 2 * speakers
    conv[...] = small[at:at + taps, :]
    at += taps
    cb[...] = small[at:at + 1, :]
    bo[...] = small[at + 1:at + 2, :]
    ls[...] = small[at + 2:at + 3, :]
    for r in range(tiles):
        bi[pl.ds(r * lanes, lanes)] = small[at + 3 + r, :]


def finish_call(meta, parts, nb, ra, rb, rs, tiles, taps, speakers):
    lanes = parts[0].shape[2]
    vm = pl.BlockSpec(memory_space=pltpu.VMEM)
    sm = pl.BlockSpec(memory_space=pltpu.SMEM)
    shapes = [(nb * lanes, tiles * lanes), (tiles * lanes, nb * lanes), (speakers, lanes), (speakers, lanes), (taps, lanes),
              (1, lanes), (1, lanes), (1, lanes), (tiles * lanes,)]
    return pl.pallas_call(
        functools.partial(finish_body, nb, ra, rb, rs, tiles, lanes, taps, speakers),
        in_specs=[sm] + [vm] * 2,
        out_specs=[vm] * len(shapes),
        out_shape=[jax.ShapeDtypeStruct(s, F32) for s in shapes],
        scratch_shapes=[pltpu.VMEM((rs * GROUP, lanes), F32)],
        name="finish",
    )(meta, *parts)


def ring(axis, size, shift):
    return lambda v: lax.ppermute(v, axis, [(i, (i + shift) % size) for i in range(size)])


def flip(axis, size, mask):
    return lambda v: lax.ppermute(v, axis, [(i, i ^ mask) for i in range(size)])


def gather_group(v, dp_count, gates):
    core = flip("dp", dp_count, 1)
    a, b = flip("dp", dp_count, 2)(v), flip("dp", dp_count, 4)(v)
    a, *one = lax.optimization_barrier((a, *gates[0]))
    c = flip("dp", dp_count, 4)(a)
    c, *two = lax.optimization_barrier((c, *gates[1]))
    return [v, core(v), a, core(a), b, core(b), c, core(c)], (one, two)


def gather_small(v, dp_count):
    near = jnp.stack([v] + [flip("dp", dp_count, 2 * m)(v) for m in range(1, GROUP // 2)])
    return [near, flip("dp", dp_count, 1)(near)]


def per_device(clips_in, speaker, counts, conv_weight, conv_bias, scale_table, shift_table,
               w_in, b_in, w_out, b_out, layer_scale, grad_out):
    clip_num, length, lanes = clips_in.shape
    nb = lax.axis_size("chan")
    dp_count = lax.axis_size("dp")
    me = lax.axis_index("chan")
    dp = lax.axis_index("dp")
    speakers = scale_table.shape[0]
    taps = conv_weight.shape[0]
    per = w_in.shape[1]
    tiles = per // lanes
    width = nb * lanes
    order = (me - jnp.arange(nb, dtype=jnp.int32)) % nb
    place = dp % GROUP
    sizes = [sum(r) for r in RUNS]
    starts = [nb * sum(sizes[:k]) for k in range(len(sizes))]
    assert clip_num == nb * sum(sizes)
    ra, rb = width // GROUP, per // GROUP
    wa = lax.dynamic_slice_in_dim(w_in, place * ra, ra).reshape(ra, tiles, lanes).transpose(1, 0, 2).reshape(-1, lanes)
    wb = lax.dynamic_slice_in_dim(w_out, place * rb, rb).reshape(rb, nb, lanes).transpose(1, 0, 2).reshape(-1, lanes)
    rows = [wa, wb, scale_table, shift_table, conv_weight, conv_bias[None], b_out[None], layer_scale[None], b_in.reshape(-1, lanes)]
    used = sum(r.shape[0] for r in rows[2:])
    small_rows = -(-used // (GROUP * 16)) * GROUP * 16
    share = jnp.pad(jnp.concatenate(rows), ((0, -used % 16), (0, 0)))
    shares = [share] + [ring("chan", nb, d)(share) for d in range(1, nb)]

    packed = []
    for start, n, runs in zip(starts, sizes, RUNS):
        low, parts = 0, []
        for run in runs:
            part = []
            for d in range(1, nb):
                at = start + (me + d) % nb * n + low
                block = jnp.stack([lax.dynamic_slice_in_dim(clips_in, at, run), lax.dynamic_slice_in_dim(grad_out, at, run)])
                part.append(ring("chan", nb, d)(block))
            parts.append(part)
            low += run
        packed.append(parts)

    stacked, prm = stack_call(shares, wa.shape[0] + wb.shape[0], 0)
    meta = jnp.stack([me, place]).astype(jnp.int32)
    gathered, packed[0] = gather_group(stacked, dp_count, packed[0])

    sums = None
    kept, back = [], []
    for k, (start, n) in enumerate(zip(starts, sizes)):
        base = start + me * n
        slot = (base + jnp.arange(n)).astype(jnp.int32)
        spk = lax.dynamic_slice_in_dim(speaker, base, n)
        live = (slot < counts[0]).astype(jnp.int32)
        out = block_call(order, spk, live, slot, meta, clips_in, grad_out, packed[k], prm, gathered, nb * per,
                         taps, speakers, small_rows, sums, HINT if k else 0)
        kept.append(out[nb:nb + 4])
        sums = out[nb + 4]
        sent = out[:nb]
        if k:
            *sent, back[0] = lax.optimization_barrier((*sent, back[0]))
        back.append([sent[0]] + [ring("chan", nb, -d)(sent[d]) for d in range(1, nb)])
    keep, send = grads_call(order, meta, *zip(*kept), sums, 2 * speakers + taps + 3)

    send, *back[0] = lax.optimization_barrier((send, *back[0]))
    got = flip("dp", dp_count, 1)(send)
    total = keep[0] + got[0].astype(F32)
    for m in range(1, GROUP // 2):
        total = total + flip("dp", dp_count, 2 * m)((keep[m] + got[m].astype(F32)).astype(BF16)).astype(F32)
    step = GROUP
    while step < dp_count:
        low = total.astype(BF16)
        total = low.astype(F32) + flip("dp", dp_count, step)(low).astype(F32)
        step *= 2
    total, back[-1] = lax.optimization_barrier((total, back[-1]))
    mine = total[0]
    for d in range(1, nb):
        mine = mine + ring("chan", nb, d)(total[d].astype(BF16)).astype(F32)
    g_in, g_out, g_scale, g_shift, g_conv, g_cb, g_bo, g_ls, g_bi = finish_call(
        meta, gather_small(mine.astype(BF16), dp_count), nb, ra, rb, small_rows // GROUP, tiles, taps, speakers)

    clips_out = jnp.zeros(clips_in.shape, BF16)
    grad_clips = grad_out.astype(F32)
    for k, n in enumerate(sizes):
        for d in range(nb):
            at = starts[k] + (me + d) % nb * n
            clips_out = lax.dynamic_update_slice_in_dim(clips_out, back[k][d][0], at, 0)
            g = lax.dynamic_slice_in_dim(grad_out, at, n).astype(F32) + back[k][d][1].astype(F32)
            grad_clips = lax.dynamic_update_slice_in_dim(grad_clips, g, at, 0)

    return (clips_out, grad_clips, g_conv, g_cb.reshape(lanes), g_scale, g_shift, g_in, g_bi, g_out,
            g_bo.reshape(lanes), g_ls.reshape(lanes))


def solution(mesh):
    act = P("dp", None, "chan")
    col, vec, row = P(None, "chan"), P("chan"), P("chan", None)
    in_specs = (act, P("dp"), P("dp"), col, vec, col, col, col, vec, row, vec, vec, act)
    out_specs = (act, act, col, vec, col, col, col, vec, row, vec, vec)
    return jax.shard_map(per_device, mesh=mesh, in_specs=in_specs, out_specs=out_specs, check_vma=False)
```

```python
import functools

import jax
import jax.numpy as jnp
from jax import lax
from jax.experimental import pallas as pl
from jax.experimental.pallas import tpu as pltpu
from jax.sharding import PartitionSpec as P

RUNS = ((1, 1), (2,))
GROUP = 8

EPS = 1e-06
ROOT_TWO_PI = 2.5066282746310002
F32 = jnp.float32
BF16 = jnp.bfloat16
PAD = 8
HINT = 1 << 36


def gelu_pair(v):
    z = jnp.abs(v)
    t = 1.0 / (1.0 + (0.3275911 * 0.7071067811865476) * z)
    e = jnp.exp(v * v * -0.5)
    poly = t * (0.5 * 0.254829592 + t * (0.5 * -0.284496736 + t * (0.5 * 1.421413741 + t * (0.5 * -1.453152027 + t * (0.5 * 1.061405429)))))
    tail = poly * e
    cdf = jnp.where(v >= 0.0, 1.0 - tail, tail)
    return v * cdf, cdf + v * (e * (1.0 / ROOT_TWO_PI))


def dot(a, b, ca, cb):
    return lax.dot_general(a, b, (((ca,), (cb,)), ((), ())), preferred_element_type=F32)


def body(n_blocks, taps, speakers, runs, first, last,
         order_ref, spk_ref, live_ref, slot_ref, meta_ref, *refs):
    nb = n_blocks
    x0, g0 = refs[:2]
    k = 2
    p = []
    for _ in runs:
        p.append(refs[k:k + nb - 1])
        k += nb - 1
    shares = refs[k:k + GROUP]
    k += GROUP
    if not first:
        got = refs[k]
        k += 1
    if last:
        before = refs[k:k + 4]
        k += 4
    o = refs[k:k + nb]
    k += nb
    if last:
        keep, send = refs[k:k + 2]
        k += 2
        (gwi, gwo, *held, sems) = refs[-7:]
    (nlow_all, blow_all, act_all, plow_all, gsm, xpad, gpad, normed, gin, slope, wide, b_in, w_in, w_out, prm) = refs[k:k + 15]
    i = pl.program_id(0)
    length, lanes = normed.shape[1], normed.shape[2]
    width = nb * lanes
    ff = act_all.shape[2]
    per = ff // nb
    tiles = per // lanes
    margin = taps // 2
    r_conv, r_cb = 2 * speakers, 2 * speakers + taps
    r_bo, r_ls, r_bi = r_cb + 1, r_cb + 2, r_cb + 3
    cols = [pl.multiple_of(order_ref[d] * lanes, lanes) for d in range(nb)]

    @pl.when(i == 0)
    def _():
        for d in range(nb):
            zero = jnp.zeros((PAD, lanes), F32)
            xpad[d, 0:PAD, :] = zero
            xpad[d, PAD + length:, :] = zero
            gpad[d, 0:PAD, :] = zero
            gpad[d, PAD + length:, :] = zero
        gsm[...] = jnp.zeros_like(gsm) if first else got[...]
        ra, rb, rs = width // GROUP, per // GROUP, prm.shape[1] // GROUP
        for s in range(GROUP):
            part = meta_ref[1] ^ s

            def unpack(d, carry):
                c = order_ref[d]
                for r in range(tiles):
                    w_in[pl.ds(pl.multiple_of(part * ra, ra), ra), pl.ds(pl.multiple_of(c * per + r * lanes, lanes), lanes)] = shares[s][d, r * ra:(r + 1) * ra, :]
                base = tiles * ra
                for r in range(nb):
                    w_out[pl.ds(pl.multiple_of(c * per + part * rb, 16), rb), r * lanes:(r + 1) * lanes] = shares[s][d, base + r * rb:base + (r + 1) * rb, :]
                base += nb * rb
                prm[d, pl.ds(pl.multiple_of(part * rs, rs), rs), :] = shares[s][d, base:base + rs, :].astype(F32)
                return carry
            lax.fori_loop(0, nb, unpack, 0)
        for d in range(nb):
            for r in range(tiles):
                at = pl.multiple_of(order_ref[d] * per + r * lanes, lanes)
                b_in[:, pl.ds(at, lanes)] = prm[d, r_bi + r:r_bi + r + 1, :]

        if last:
            for j in range(4):
                pltpu.make_async_copy(before[j], held[j], sems.at[j]).start()

    row = i if last else 0
    nlow, blow, act, plow = (v.at[row] for v in (nlow_all, blow_all, act_all, plow_all))
    xpad[0, PAD:PAD + length, :] = x0[0].astype(F32)
    gin[0] = g0[0]
    low = 0
    for run, part in zip(runs, p):
        @pl.when((i >= low) & (i < low + run))
        def _(low=low, run=run, part=part):
            at = i - low if run > 1 else 0
            for d in range(1, nb):
                xpad[d, PAD:PAD + length, :] = part[d - 1][0, at].astype(F32)
                gin[d] = part[d - 1][1, at]
        low += run

    spk = spk_ref[i]
    live = live_ref[i].astype(F32)
    total = jnp.zeros((length, 1), F32)
    for d in range(nb):
        acc = jnp.broadcast_to(prm[d, r_cb:r_cb + 1, :], (length, lanes))
        for t in range(taps):
            s = PAD - margin + t
            acc = acc + prm[d, r_conv + t:r_conv + t + 1, :] * xpad[d, s:s + length, :]
        normed[d] = acc
        total = total + jnp.sum(acc, 1, keepdims=True)
    mean = total / width
    square = jnp.zeros((length, 1), F32)
    for d in range(nb):
        c = normed[d] - mean
        normed[d] = c
        square = square + jnp.sum(c * c, 1, keepdims=True)
    inv = lax.rsqrt(square / width + EPS)
    for d in range(nb):
        v = normed[d] * inv
        normed[d] = v
        sc = prm[d, pl.ds(spk, 1), :]
        sh = prm[d, pl.ds(speakers + spk, 1), :]
        nlow[:, pl.ds(cols[d], lanes)] = (v * sc + sh).astype(BF16)

    step = 256
    for f in range(0, ff, step):
        pre = dot(nlow[...], w_in[:, f:f + step], 1, 0) + b_in[:, f:f + step]
        a, s = gelu_pair(pre)
        act[:, f:f + step] = a.astype(BF16)
        slope[:, f:f + step] = s
    wide[...] = dot(act[...], w_out[...], 1, 0)
    for d in range(nb):
        b = wide[:, pl.ds(cols[d], lanes)] + prm[d, r_bo:r_bo + 1, :]
        ls = prm[d, r_ls:r_ls + 1, :] * live
        x = xpad[d, PAD:PAD + length, :]
        g = gin[d].astype(F32)
        o[d][0, 0] = (x + b * ls).astype(BF16)
        gb = g * ls
        gsm[d, r_bo:r_bo + 1, :] += jnp.sum(gb, 0, keepdims=True)
        gsm[d, r_ls:r_ls + 1, :] += jnp.sum(g * b, 0, keepdims=True) * live
        blow[:, pl.ds(cols[d], lanes)] = gb.astype(BF16)
    for f in range(0, ff, step):
        gp = dot(blow[...], w_out[f:f + step, :], 1, 1) * slope[:, f:f + step]
        plow[:, f:f + step] = gp.astype(BF16)
        gsum = jnp.sum(gp, 0, keepdims=True)
        for r in range(step // lanes):
            q = f // lanes + r
            gsm[nb, q:q + 1, :] += gsum[:, r * lanes:(r + 1) * lanes]
    wide[...] = dot(plow[...], w_in[...], 1, 1)
    m1 = jnp.zeros((length, 1), F32)
    m2 = jnp.zeros((length, 1), F32)
    for d in range(nb):
        gn = wide[:, pl.ds(cols[d], lanes)]
        v = normed[d]
        gv = gn * v
        gsm[d, pl.ds(spk, 1), :] += jnp.sum(gv, 0, keepdims=True)
        gsm[d, pl.ds(speakers + spk, 1), :] += jnp.sum(gn, 0, keepdims=True)
        sc = prm[d, pl.ds(spk, 1), :]
        m1 = m1 + jnp.sum(gn * sc, 1, keepdims=True)
        m2 = m2 + jnp.sum(gv * sc, 1, keepdims=True)
    m1 = m1 / width
    m2 = m2 / width
    for d in range(nb):
        sc = prm[d, pl.ds(spk, 1), :]
        gc = (wide[:, pl.ds(cols[d], lanes)] * sc - m1 - normed[d] * m2) * inv
        gpad[d, PAD:PAD + length, :] = gc
        gsm[d, r_cb:r_cb + 1, :] += jnp.sum(gc, 0, keepdims=True)
        acc = jnp.zeros((length, lanes), F32)
        for t in range(taps):
            s = PAD - margin + t
            gsm[d, r_conv + t:r_conv + t + 1, :] += jnp.sum(xpad[d, s:s + length, :] * gc, 0, keepdims=True)
            s = PAD + margin - t
            acc = acc + prm[d, r_conv + t:r_conv + t + 1, :] * gpad[d, s:s + length, :]
        o[d][1, 0] = acc.astype(BF16)

    if last:
        @pl.when(i == pl.num_programs(0) - 1)
        def _():
            for j in range(4):
                pltpu.make_async_copy(before[j], held[j], sems.at[j]).wait()
            flat = [v[...].reshape(-1, v.shape[2]) for v in (nlow_all, blow_all)]
            heads = [v[...].reshape(-1, v.shape[2]) for v in held[:2]]
            for f in range(0, ff, step):
                cut = lambda v: v[:, :, f:f + step].reshape(-1, step)
                da = dot(flat[0], cut(plow_all), 0, 0) + dot(heads[0], cut(held[3]), 0, 0)
                for r in range(step // lanes):
                    gwi[f // lanes + r] = da[:, r * lanes:(r + 1) * lanes]
                gwo[f:f + step, :] = dot(cut(act_all), flat[1], 0, 0) + dot(cut(held[2]), heads[1], 0, 0)
            for d in range(nb):
                for r in range(tiles):
                    gsm[d, r_bi + r:r_bi + r + 1, :] = gsm[nb, pl.ds(order_ref[d] * tiles + r, 1), :]
            place = meta_ref[1]
            ra, rb, rs = width // GROUP, per // GROUP, gsm.shape[1] // GROUP

            def emit(m, carry):
                for e in range(nb):
                    d = -e % nb
                    c = order_ref[d]
                    for out, part in ((keep, place ^ (2 * m)), (send, place ^ (2 * m) ^ 1)):
                        for r in range(tiles):
                            v = gwi[c * tiles + r, pl.ds(pl.multiple_of(part * ra, ra), ra), :]
                            out[m, e, r * ra:(r + 1) * ra, :] = v.astype(out.dtype)
                        base = tiles * ra
                        for r in range(nb):
                            v = gwo[pl.ds(pl.multiple_of(c * per + part * rb, 16), rb), r * lanes:(r + 1) * lanes]
                            out[m, e, base + r * rb:base + (r + 1) * rb, :] = v.astype(out.dtype)
                        base += nb * rb
                        v = gsm[d, pl.ds(pl.multiple_of(part * rs, rs), rs), :]
                        out[m, e, base:base + rs, :] = v.astype(out.dtype)
                return carry
            lax.fori_loop(0, GROUP // 2, emit, 0)


def block_call(order, spk, live, slot, meta, clips, grads, packed, shares, ff, taps, speakers, small_rows, carried, before):
    nb = len(packed[0]) + 1
    runs = [part[0].shape[1] for part in packed]
    n = sum(runs)
    _, _, length, lanes = packed[0][0].shape
    width = nb * lanes
    first, last = carried is None, before is not None
    per = ff // nb
    rows = (width // GROUP) * (per // lanes) + (per // GROUP) * nb + small_rows // GROUP
    widths = (width, width, ff, ff)
    full = lambda shape: pl.BlockSpec(shape, lambda i, *_: (0,) * len(shape), pipeline_mode=pl.Buffered(1))
    step = lambda *shape: pl.BlockSpec((1,) + shape, lambda i, *_: (i,) + (0,) * len(shape))
    own = pl.BlockSpec((1, length, lanes), lambda i, order, spk, live, slot, meta: (slot[i], 0, 0))
    sums = (nb + 1, small_rows, lanes)
    args = [clips, grads] + [v for part in packed for v in part] + list(shares)
    in_specs = [own, own] + [full(v.shape) for v in args[2:]]
    out_shape = [jax.ShapeDtypeStruct((2, n, length, lanes), BF16)] * nb
    out_specs = [pl.BlockSpec((2, 1, length, lanes), lambda i, *_: (0, i, 0, 0))] * nb
    if not first:
        args.append(carried)
        in_specs.append(full(sums))
    if last:
        args += list(before)
        in_specs += [pl.BlockSpec(memory_space=pl.ANY)] * 4
        out_shape += [jax.ShapeDtypeStruct((GROUP // 2, nb, rows, lanes), BF16)] * 2
        out_specs += [pl.BlockSpec((GROUP // 2, nb, rows, lanes), lambda i, *_: (0, 0, 0, 0))] * 2
    else:
        out_shape += [jax.ShapeDtypeStruct((n, length, w), BF16) for w in widths] + [jax.ShapeDtypeStruct(sums, F32)]
        out_specs += [step(length, w) for w in widths] + [pl.BlockSpec(sums, lambda i, *_: (0, 0, 0))]
    scratch = [
        pltpu.VMEM((nb, length + 2 * PAD, lanes), F32),
        pltpu.VMEM((nb, length + 2 * PAD, lanes), F32),
        pltpu.VMEM((nb, length, lanes), F32),
        pltpu.VMEM((nb, length, lanes), BF16),
        pltpu.VMEM((length, ff), F32),
        pltpu.VMEM((length, width), F32),
        pltpu.VMEM((1, ff), F32),
        pltpu.VMEM((width, ff), BF16),
        pltpu.VMEM((ff, width), BF16),
        pltpu.VMEM((nb, small_rows, lanes), F32),
    ]
    if last:
        scratch = [pltpu.VMEM((n, length, w), BF16) for w in widths] + [pltpu.VMEM(sums, F32)] + scratch
        scratch += [pltpu.VMEM((ff // lanes, width, lanes), F32), pltpu.VMEM((ff, width), F32)]
        scratch += [pltpu.VMEM(v.shape, BF16) for v in before] + [pltpu.SemaphoreType.DMA((4,))]
    return pl.pallas_call(
        functools.partial(body, nb, taps, speakers, runs, first, last),
        out_shape=out_shape,
        grid_spec=pltpu.PrefetchScalarGridSpec(
            num_scalar_prefetch=5, grid=(n,), in_specs=in_specs, out_specs=out_specs, scratch_shapes=scratch),
        cost_estimate=pl.CostEstimate(flops=HINT if last else 0, transcendentals=0, bytes_accessed=0),
        compiler_params=pltpu.CompilerParams(dimension_semantics=("arbitrary",), vmem_limit_bytes=60 << 20),
        name="block",
    )(order, spk, live, slot, meta, *args)


def pack_body(moves, slot_ref, clips, grads, *refs):
    blocks, sems = refs[:-1], refs[-1]
    copies = []
    for j, (at, r, source) in enumerate(moves):
        for q, array in enumerate((clips, grads)):
            copies.append(pltpu.make_async_copy(array.at[slot_ref[source]], blocks[at].at[q, r], sems.at[2 * j + q]))
    for copy in copies:
        copy.start()
    for copy in copies:
        copy.wait()


def pack_call(slots, blocks, clips, grads):
    length, lanes = clips.shape[1:]
    moves, source = [], 0
    for at, run in enumerate(blocks):
        for r in range(run):
            moves.append((at, r, source))
            source += 1
    hbm = pl.BlockSpec(memory_space=pl.ANY)
    sm = pl.BlockSpec(memory_space=pltpu.SMEM)
    vm = pl.BlockSpec(memory_space=pltpu.VMEM)
    return pl.pallas_call(
        functools.partial(pack_body, moves),
        out_shape=[jax.ShapeDtypeStruct((2, run, length, lanes), BF16) for run in blocks],
        in_specs=[sm, hbm, hbm],
        out_specs=[vm] * len(blocks),
        scratch_shapes=[pltpu.SemaphoreType.DMA((2 * len(moves),))],
        name="pack",
    )(slots, clips, grads)


def share_body(taps, speakers, place_ref, w_in, w_out, scale, shift, conv, cb, bo, ls, bi, share, small):
    lanes = share.shape[1]
    small[0:speakers, :] = scale[...].astype(F32)
    small[speakers:2 * speakers, :] = shift[...].astype(F32)
    at = 2 * speakers
    small[at:at + taps, :] = conv[...].astype(F32)
    at += taps
    for v in (cb, bo, ls):
        small[at, :] = v[...].astype(F32)
        at += 1
    tiles = bi.shape[0] // lanes
    for r in range(tiles):
        small[at + r, :] = bi[pl.ds(r * lanes, lanes)].astype(F32)
    at += tiles
    small[at:, :] = jnp.zeros((small.shape[0] - at, lanes), F32)
    ra, rb, rs = w_in.shape[0], w_out.shape[0], small.shape[0] // GROUP
    for r in range(tiles):
        share[r * ra:(r + 1) * ra, :] = w_in[:, r * lanes:(r + 1) * lanes]
    base = tiles * ra
    for r in range(w_out.shape[1] // lanes):
        share[base + r * rb:base + (r + 1) * rb, :] = w_out[:, r * lanes:(r + 1) * lanes]
    base += w_out.shape[1] // lanes * rb
    share[base:base + rs, :] = small[pl.ds(pl.multiple_of(place_ref[0] * rs, rs), rs), :].astype(BF16)


def share_call(place, w_in, w_out, small, small_rows):
    lanes = small[0].shape[1]
    speakers, taps = small[0].shape[0], small[2].shape[0]
    ra, rb = w_in.shape[0] // GROUP, w_out.shape[0] // GROUP
    rows = w_in.shape[1] // lanes * ra + w_out.shape[1] // lanes * rb + small_rows // GROUP
    full = lambda shape: pl.BlockSpec(shape, lambda i, *_: (0,) * len(shape))
    share_row = lambda shape: pl.BlockSpec(shape, lambda i, place: (place[0], 0))
    return pl.pallas_call(
        functools.partial(share_body, taps, speakers),
        out_shape=jax.ShapeDtypeStruct((rows, lanes), BF16),
        grid_spec=pltpu.PrefetchScalarGridSpec(
            num_scalar_prefetch=1, grid=(1,),
            in_specs=[share_row((ra, w_in.shape[1])), share_row((rb, w_out.shape[1]))] + [full(v.shape) for v in small],
            out_specs=full((rows, lanes)),
            scratch_shapes=[pltpu.VMEM((small_rows, lanes), F32)]),
        compiler_params=pltpu.CompilerParams(dimension_semantics=("arbitrary",)),
        name="share",
    )(place, w_in, w_out, *small)


def stack_body(*refs):
    for d, v in enumerate(refs[:-1]):
        refs[-1][d] = v[...]


def stack_call(parts):
    return pl.pallas_call(
        stack_body,
        out_shape=jax.ShapeDtypeStruct((len(parts),) + parts[0].shape, BF16),
        name="gathered",
    )(*parts)


def finish_body(nb, ra, rb, rs, tiles, lanes, taps, speakers, meta_ref, *refs):
    ins = [refs[s % 2].at[s // 2] for s in range(GROUP)]
    g_in, g_out, scale, shift, conv, cb, bo, ls, bi, small = refs[2:]
    for s in range(GROUP):
        part = meta_ref[1] ^ s
        for r in range(tiles):
            g_in[pl.ds(pl.multiple_of(part * ra, ra), ra), r * lanes:(r + 1) * lanes] = ins[s][r * ra:(r + 1) * ra, :].astype(F32)
        base = tiles * ra
        for r in range(nb):
            g_out[pl.ds(pl.multiple_of(part * rb, 16), rb), r * lanes:(r + 1) * lanes] = ins[s][base + r * rb:base + (r + 1) * rb, :].astype(F32)
        base += nb * rb
        small[pl.ds(pl.multiple_of(part * rs, rs), rs), :] = ins[s][base:base + rs, :].astype(F32)
    scale[...] = small[0:speakers, :]
    shift[...] = small[speakers:2 * speakers, :]
    at = 2 * speakers
    conv[...] = small[at:at + taps, :]
    at += taps
    cb[...] = small[at:at + 1, :]
    bo[...] = small[at + 1:at + 2, :]
    ls[...] = small[at + 2:at + 3, :]
    for r in range(tiles):
        bi[pl.ds(r * lanes, lanes)] = small[at + 3 + r, :]


def finish_call(meta, parts, nb, ra, rb, rs, tiles, taps, speakers):
    lanes = parts[0].shape[2]
    vm = pl.BlockSpec(memory_space=pltpu.VMEM)
    sm = pl.BlockSpec(memory_space=pltpu.SMEM)
    shapes = [(nb * lanes, tiles * lanes), (tiles * lanes, nb * lanes), (speakers, lanes), (speakers, lanes), (taps, lanes),
              (1, lanes), (1, lanes), (1, lanes), (tiles * lanes,)]
    return pl.pallas_call(
        functools.partial(finish_body, nb, ra, rb, rs, tiles, lanes, taps, speakers),
        in_specs=[sm] + [vm] * 2,
        out_specs=[vm] * len(shapes),
        out_shape=[jax.ShapeDtypeStruct(s, F32) for s in shapes],
        scratch_shapes=[pltpu.VMEM((rs * GROUP, lanes), F32)],
        name="finish",
    )(meta, *parts)


def ring(axis, size, shift):
    return lambda v: lax.ppermute(v, axis, [(i, (i + shift) % size) for i in range(size)])


def flip(axis, size, mask):
    return lambda v: lax.ppermute(v, axis, [(i, i ^ mask) for i in range(size)])


def gather_group(v, dp_count, gates):
    core = flip("dp", dp_count, 1)
    a, b = flip("dp", dp_count, 2)(v), flip("dp", dp_count, 4)(v)
    a, *one = lax.optimization_barrier((a, *gates[0]))
    c = flip("dp", dp_count, 4)(a)
    c, *two = lax.optimization_barrier((c, *gates[1]))
    return [v, core(v), a, core(a), b, core(b), c, core(c)], (one, two)


def gather_small(v, dp_count):
    near = jnp.stack([v] + [flip("dp", dp_count, 2 * m)(v) for m in range(1, GROUP // 2)])
    return [near, flip("dp", dp_count, 1)(near)]


def per_device(clips_in, speaker, counts, conv_weight, conv_bias, scale_table, shift_table,
               w_in, b_in, w_out, b_out, layer_scale, grad_out):
    clip_num, length, lanes = clips_in.shape
    nb = lax.axis_size("chan")
    dp_count = lax.axis_size("dp")
    me = lax.axis_index("chan")
    dp = lax.axis_index("dp")
    speakers = scale_table.shape[0]
    taps = conv_weight.shape[0]
    per = w_in.shape[1]
    tiles = per // lanes
    width = nb * lanes
    order = (me - jnp.arange(nb, dtype=jnp.int32)) % nb
    place = dp % GROUP
    sizes = [sum(r) for r in RUNS]
    starts = [nb * sum(sizes[:k]) for k in range(len(sizes))]
    assert clip_num == nb * sum(sizes)
    ra, rb = width // GROUP, per // GROUP
    small = [scale_table, shift_table, conv_weight, conv_bias, b_out, layer_scale, b_in]
    used = 2 * speakers + taps + 3 + tiles
    small_rows = -(-used // (GROUP * 16)) * GROUP * 16
    slots, blocks = [], []
    for start, n, runs in zip(starts, sizes, RUNS):
        low = 0
        for run in runs:
            for d in range(1, nb):
                blocks.append(run)
                slots.append(start + (me + d) % nb * n + low + jnp.arange(run))
            low += run
    share = share_call(place.astype(jnp.int32)[None], w_in, w_out, small, small_rows)
    packed = pack_call(jnp.concatenate(slots).astype(jnp.int32), blocks, clips_in, grad_out)

    shares = [share] + [ring("chan", nb, d)(share) for d in range(1, nb)]
    stacked = stack_call(shares)
    stacked, *packed = lax.optimization_barrier((stacked, *packed))
    came = [ring("chan", nb, 1 + j % (nb - 1))(v) for j, v in enumerate(packed)]
    packed = []
    for runs in RUNS:
        packed.append([])
        for _ in runs:
            packed[-1].append(came[:nb - 1])
            came = came[nb - 1:]
    meta = jnp.stack([me, place]).astype(jnp.int32)
    gathered, packed[0] = gather_group(stacked, dp_count, packed[0])

    sums, kept, back = None, None, []
    for k, (start, n) in enumerate(zip(starts, sizes)):
        base = start + me * n
        slot = (base + jnp.arange(n)).astype(jnp.int32)
        spk = lax.dynamic_slice_in_dim(speaker, base, n)
        live = (slot < counts[0]).astype(jnp.int32)
        out = block_call(order, spk, live, slot, meta, clips_in, grad_out, packed[k], gathered, nb * per,
                         taps, speakers, small_rows, sums, kept)
        if k:
            keep, send = out[nb:]
        else:
            kept, sums = out[nb:nb + 4], out[nb + 4]
        sent = out[:nb]
        if k:
            sent, back[0] = lax.optimization_barrier((sent, back[0]))
        else:
            sent, packed[1] = lax.optimization_barrier((sent, packed[1]))
        back.append([sent[0]] + [ring("chan", nb, -d)(sent[d]) for d in range(1, nb)])

    send, *back[0] = lax.optimization_barrier((send, *back[0]))
    got = flip("dp", dp_count, 1)(send)
    total = keep[0].astype(F32) + got[0].astype(F32)
    outward = [(keep[m].astype(F32) + got[m].astype(F32)).astype(BF16) for m in range(1, GROUP // 2)]
    outward, back[0] = lax.optimization_barrier((outward, back[0]))
    for m in range(1, GROUP // 2):
        total = total + flip("dp", dp_count, 2 * m)(outward[m - 1]).astype(F32)
    step = GROUP
    while step < dp_count:
        low = total.astype(BF16)
        total = low.astype(F32) + flip("dp", dp_count, step)(low).astype(F32)
        step *= 2
    total, back[-1] = lax.optimization_barrier((total, back[-1]))
    mine = total[0]
    for d in range(1, nb):
        mine = mine + ring("chan", nb, d)(total[d].astype(BF16)).astype(F32)
    clips_out = jnp.zeros(clips_in.shape, BF16)
    grad_clips = grad_out.astype(F32)
    for k, n in enumerate(sizes):
        for d in range(nb):
            at = starts[k] + (me + d) % nb * n
            clips_out = lax.dynamic_update_slice_in_dim(clips_out, back[k][d][0], at, 0)
            g = lax.dynamic_slice_in_dim(grad_out, at, n).astype(F32) + back[k][d][1].astype(F32)
            grad_clips = lax.dynamic_update_slice_in_dim(grad_clips, g, at, 0)
    mine, clips_out, grad_clips = lax.optimization_barrier((mine, clips_out, grad_clips))

    g_in, g_out, g_scale, g_shift, g_conv, g_cb, g_bo, g_ls, g_bi = finish_call(
        meta, gather_small(mine.astype(BF16), dp_count), nb, ra, rb, small_rows // GROUP, tiles, taps, speakers)

    return (clips_out, grad_clips, g_conv, g_cb.reshape(lanes), g_scale, g_shift, g_in, g_bi, g_out,
            g_bo.reshape(lanes), g_ls.reshape(lanes))


def solution(mesh):
    act = P("dp", None, "chan")
    col, vec, row = P(None, "chan"), P("chan"), P("chan", None)
    in_specs = (act, P("dp"), P("dp"), col, vec, col, col, col, vec, row, vec, vec, act)
    out_specs = (act, act, col, vec, col, col, col, vec, row, vec, vec)
    return jax.shard_map(per_device, mesh=mesh, in_specs=in_specs, out_specs=out_specs, check_vma=False)
```

```python
import functools

import jax
import jax.numpy as jnp
from jax import lax
from jax.experimental import pallas as pl
from jax.experimental.pallas import tpu as pltpu
from jax.sharding import PartitionSpec as P

RUNS = ((1, 1), (2,))
GROUP = 8
GATED = True

EPS = 1e-06
ROOT_TWO_PI = 2.5066282746310002
F32 = jnp.float32
BF16 = jnp.bfloat16
PAD = 8
HINT = 1 << 36


def gelu_pair(v):
    z = jnp.abs(v)
    t = 1.0 / (1.0 + (0.3275911 * 0.7071067811865476) * z)
    e = jnp.exp(v * v * -0.5)
    poly = t * (0.5 * 0.254829592 + t * (0.5 * -0.284496736 + t * (0.5 * 1.421413741 + t * (0.5 * -1.453152027 + t * (0.5 * 1.061405429)))))
    tail = poly * e
    cdf = jnp.where(v >= 0.0, 1.0 - tail, tail)
    return v * cdf, cdf + v * (e * (1.0 / ROOT_TWO_PI))


def dot(a, b, ca, cb):
    return lax.dot_general(a, b, (((ca,), (cb,)), ((), ())), preferred_element_type=F32)


class Order:
    def __init__(self, me, count):
        self.me, self.count = me, count

    def __getitem__(self, d):
        return lax.rem(self.me + self.count - d, self.count)


def body(n_blocks, taps, speakers, runs, first, last, each, first_slot,
         meta_ref, spk_ref, count_ref, *refs):
    nb = n_blocks
    order_ref = Order(meta_ref[0], nb)
    x0, g0 = refs[:2]
    k = 2
    p = []
    for _ in runs:
        p.append(refs[k:k + nb - 1])
        k += nb - 1
    if first:
        shares = [refs[k + s % 2].at[s // 2] for s in range(GROUP)]
        k += 2
    else:
        w_in, w_out, prm = refs[k:k + 3]
        k += 3
    if not first:
        got = refs[k]
        k += 1
    if last:
        before = refs[k:k + 4]
        k += 4
    o = refs[k:k + nb]
    k += nb
    if last:
        keep, send = refs[k:k + 2]
        k += 2
        (gwi, gwo, *held, sems) = refs[-7:]
    (nlow_all, blow_all, act_all, plow_all, gsm, *refs) = refs[k:]
    if first:
        w_in, w_out, prm, *refs = refs
    xpad, gpad, normed, gin, slope, wide, b_in = refs[:7]
    i = pl.program_id(0)
    length, lanes = normed.shape[1], normed.shape[2]
    width = nb * lanes
    ff = act_all.shape[2]
    per = ff // nb
    tiles = per // lanes
    margin = taps // 2
    r_conv, r_cb = 2 * speakers, 2 * speakers + taps
    r_bo, r_ls, r_bi = r_cb + 1, r_cb + 2, r_cb + 3
    cols = [pl.multiple_of(order_ref[d] * lanes, lanes) for d in range(nb)]

    @pl.when(i == 0)
    def _():
        for d in range(nb):
            zero = jnp.zeros((PAD, lanes), F32)
            xpad[d, 0:PAD, :] = zero
            xpad[d, PAD + length:, :] = zero
            gpad[d, 0:PAD, :] = zero
            gpad[d, PAD + length:, :] = zero
        gsm[...] = jnp.zeros_like(gsm) if first else got[...]
        if first:
            ra, rb, rs = width // GROUP, per // GROUP, prm.shape[1] // GROUP
            for s in range(GROUP):
                part = meta_ref[1] ^ s

                def unpack(d, carry):
                    c = order_ref[d]
                    for r in range(tiles):
                        w_in[pl.ds(pl.multiple_of(part * ra, ra), ra), pl.ds(pl.multiple_of(c * per + r * lanes, lanes), lanes)] = shares[s][d, r * ra:(r + 1) * ra, :]
                    base = tiles * ra
                    for r in range(nb):
                        w_out[pl.ds(pl.multiple_of(c * per + part * rb, 16), rb), r * lanes:(r + 1) * lanes] = shares[s][d, base + r * rb:base + (r + 1) * rb, :]
                    base += nb * rb
                    prm[d, pl.ds(pl.multiple_of(part * rs, rs), rs), :] = shares[s][d, base:base + rs, :].astype(F32)
                    return carry
                lax.fori_loop(0, nb, unpack, 0)
        for d in range(nb):
            for r in range(tiles):
                at = pl.multiple_of(order_ref[d] * per + r * lanes, lanes)
                b_in[:, pl.ds(at, lanes)] = prm[d, r_bi + r:r_bi + r + 1, :]

        if last:
            for j in range(4):
                pltpu.make_async_copy(before[j], held[j], sems.at[j]).start()

    row = i if last else 0
    nlow, blow, act, plow = (v.at[row] for v in (nlow_all, blow_all, act_all, plow_all))
    xpad[0, PAD:PAD + length, :] = x0[0].astype(F32)
    gin[0] = g0[0]
    low = 0
    for run, part in zip(runs, p):
        @pl.when((i >= low) & (i < low + run))
        def _(low=low, run=run, part=part):
            at = i - low if run > 1 else 0
            for d in range(1, nb):
                xpad[d, PAD:PAD + length, :] = part[d - 1][0, at].astype(F32)
                gin[d] = part[d - 1][1, at]
        low += run

    slot = meta_ref[0] * each + first_slot + i
    spk = spk_ref[slot]
    live = (slot < count_ref[0]).astype(F32)
    total = jnp.zeros((length, 1), F32)
    for d in range(nb):
        acc = jnp.broadcast_to(prm[d, r_cb:r_cb + 1, :], (length, lanes))
        for t in range(taps):
            s = PAD - margin + t
            acc = acc + prm[d, r_conv + t:r_conv + t + 1, :] * xpad[d, s:s + length, :]
        normed[d] = acc
        total = total + jnp.sum(acc, 1, keepdims=True)
    mean = total / width
    square = jnp.zeros((length, 1), F32)
    for d in range(nb):
        c = normed[d] - mean
        normed[d] = c
        square = square + jnp.sum(c * c, 1, keepdims=True)
    inv = lax.rsqrt(square / width + EPS)
    for d in range(nb):
        v = normed[d] * inv
        normed[d] = v
        sc = prm[d, pl.ds(spk, 1), :]
        sh = prm[d, pl.ds(speakers + spk, 1), :]
        nlow[:, pl.ds(cols[d], lanes)] = (v * sc + sh).astype(BF16)

    step = 256
    for f in range(0, ff, step):
        pre = dot(nlow[...], w_in[:, f:f + step], 1, 0) + b_in[:, f:f + step]
        a, s = gelu_pair(pre)
        act[:, f:f + step] = a.astype(BF16)
        slope[:, f:f + step] = s
    wide[...] = dot(act[...], w_out[...], 1, 0)
    for d in range(nb):
        b = wide[:, pl.ds(cols[d], lanes)] + prm[d, r_bo:r_bo + 1, :]
        ls = prm[d, r_ls:r_ls + 1, :] * live
        x = xpad[d, PAD:PAD + length, :]
        g = gin[d].astype(F32)
        o[d][0, 0] = (x + b * ls).astype(BF16)
        gb = g * ls
        gsm[d, r_bo:r_bo + 1, :] += jnp.sum(gb, 0, keepdims=True)
        gsm[d, r_ls:r_ls + 1, :] += jnp.sum(g * b, 0, keepdims=True) * live
        blow[:, pl.ds(cols[d], lanes)] = gb.astype(BF16)
    for f in range(0, ff, step):
        gp = dot(blow[...], w_out[f:f + step, :], 1, 1) * slope[:, f:f + step]
        plow[:, f:f + step] = gp.astype(BF16)
        gsum = jnp.sum(gp, 0, keepdims=True)
        for r in range(step // lanes):
            q = f // lanes + r
            gsm[nb, q:q + 1, :] += gsum[:, r * lanes:(r + 1) * lanes]
    wide[...] = dot(plow[...], w_in[...], 1, 1)
    m1 = jnp.zeros((length, 1), F32)
    m2 = jnp.zeros((length, 1), F32)
    for d in range(nb):
        gn = wide[:, pl.ds(cols[d], lanes)]
        v = normed[d]
        gv = gn * v
        gsm[d, pl.ds(spk, 1), :] += jnp.sum(gv, 0, keepdims=True)
        gsm[d, pl.ds(speakers + spk, 1), :] += jnp.sum(gn, 0, keepdims=True)
        sc = prm[d, pl.ds(spk, 1), :]
        m1 = m1 + jnp.sum(gn * sc, 1, keepdims=True)
        m2 = m2 + jnp.sum(gv * sc, 1, keepdims=True)
    m1 = m1 / width
    m2 = m2 / width
    for d in range(nb):
        sc = prm[d, pl.ds(spk, 1), :]
        gc = (wide[:, pl.ds(cols[d], lanes)] * sc - m1 - normed[d] * m2) * inv
        gpad[d, PAD:PAD + length, :] = gc
        gsm[d, r_cb:r_cb + 1, :] += jnp.sum(gc, 0, keepdims=True)
        acc = jnp.zeros((length, lanes), F32)
        for t in range(taps):
            s = PAD - margin + t
            gsm[d, r_conv + t:r_conv + t + 1, :] += jnp.sum(xpad[d, s:s + length, :] * gc, 0, keepdims=True)
            s = PAD + margin - t
            acc = acc + prm[d, r_conv + t:r_conv + t + 1, :] * gpad[d, s:s + length, :]
        o[d][1, 0] = acc.astype(BF16)

    if last:
        @pl.when(i == pl.num_programs(0) - 1)
        def _():
            for j in range(4):
                pltpu.make_async_copy(before[j], held[j], sems.at[j]).wait()
            flat = [v[...].reshape(-1, v.shape[2]) for v in (nlow_all, blow_all)]
            heads = [v[...].reshape(-1, v.shape[2]) for v in held[:2]]
            for f in range(0, ff, step):
                cut = lambda v: v[:, :, f:f + step].reshape(-1, step)
                da = dot(flat[0], cut(plow_all), 0, 0) + dot(heads[0], cut(held[3]), 0, 0)
                for r in range(step // lanes):
                    gwi[f // lanes + r] = da[:, r * lanes:(r + 1) * lanes]
                gwo[f:f + step, :] = dot(cut(act_all), flat[1], 0, 0) + dot(cut(held[2]), heads[1], 0, 0)
            for d in range(nb):
                for r in range(tiles):
                    gsm[d, r_bi + r:r_bi + r + 1, :] = gsm[nb, pl.ds(order_ref[d] * tiles + r, 1), :]
            place = meta_ref[1]
            ra, rb, rs = width // GROUP, per // GROUP, gsm.shape[1] // GROUP

            def emit(m, carry):
                for e in range(nb):
                    d = -e % nb
                    c = order_ref[d]
                    for out, part in ((keep, place ^ (2 * m)), (send, place ^ (2 * m) ^ 1)):
                        for r in range(tiles):
                            v = gwi[c * tiles + r, pl.ds(pl.multiple_of(part * ra, ra), ra), :]
                            out[m, e, r * ra:(r + 1) * ra, :] = v.astype(out.dtype)
                        base = tiles * ra
                        for r in range(nb):
                            v = gwo[pl.ds(pl.multiple_of(c * per + part * rb, 16), rb), r * lanes:(r + 1) * lanes]
                            out[m, e, base + r * rb:base + (r + 1) * rb, :] = v.astype(out.dtype)
                        base += nb * rb
                        v = gsm[d, pl.ds(pl.multiple_of(part * rs, rs), rs), :]
                        out[m, e, base:base + rs, :] = v.astype(out.dtype)
                return carry
            lax.fori_loop(0, GROUP // 2, emit, 0)


def block_call(meta, speaker, counts, low, clips, grads, packed, shares, ff, taps, speakers, small_rows, carried, before):
    nb = len(packed[0]) + 1
    runs = [part[0].shape[1] for part in packed]
    n = sum(runs)
    each = clips.shape[0] // nb
    _, _, length, lanes = packed[0][0].shape
    width = nb * lanes
    first, last = carried is None, before is not None
    per = ff // nb
    rows = (width // GROUP) * (per // lanes) + (per // GROUP) * nb + small_rows // GROUP
    widths = (width, width, ff, ff)
    full = lambda shape: pl.BlockSpec(shape, lambda i, *_: (0,) * len(shape), pipeline_mode=pl.Buffered(1))
    step = lambda *shape: pl.BlockSpec((1,) + shape, lambda i, *_: (i,) + (0,) * len(shape))
    own = pl.BlockSpec((1, length, lanes), lambda i, meta, *_: (meta[0] * each + low + i, 0, 0))
    sums = (nb + 1, small_rows, lanes)
    args = [clips, grads] + [v for part in packed for v in part] + list(shares)
    in_specs = [own, own] + [full(v.shape) for v in args[2:]]
    out_shape = [jax.ShapeDtypeStruct((2, n, length, lanes), BF16)] * nb
    out_specs = [pl.BlockSpec((2, 1, length, lanes), lambda i, *_: (0, i, 0, 0))] * nb
    if not first:
        args.append(carried)
        in_specs.append(full(sums))
    if last:
        args += list(before)
        in_specs += [pl.BlockSpec(memory_space=pl.ANY)] * 4
        out_shape += [jax.ShapeDtypeStruct((GROUP // 2, nb, rows, lanes), BF16)] * 2
        out_specs += [pl.BlockSpec((GROUP // 2, nb, rows, lanes), lambda i, *_: (0, 0, 0, 0))] * 2
    else:
        out_shape += [jax.ShapeDtypeStruct((n, length, w), BF16) for w in widths] + [jax.ShapeDtypeStruct(sums, F32)]
        out_specs += [step(length, w) for w in widths] + [pl.BlockSpec(sums, lambda i, *_: (0, 0, 0))]
        weights = [((width, ff), BF16), ((ff, width), BF16), ((nb, small_rows, lanes), F32)]
        out_shape += [jax.ShapeDtypeStruct(shape, t) for shape, t in weights]
        out_specs += [full(shape) for shape, _ in weights]
    scratch = [
        pltpu.VMEM((nb, length + 2 * PAD, lanes), F32),
        pltpu.VMEM((nb, length + 2 * PAD, lanes), F32),
        pltpu.VMEM((nb, length, lanes), F32),
        pltpu.VMEM((nb, length, lanes), BF16),
        pltpu.VMEM((length, ff), F32),
        pltpu.VMEM((length, width), F32),
        pltpu.VMEM((1, ff), F32),
    ]
    if last:
        scratch = [pltpu.VMEM((n, length, w), BF16) for w in widths] + [pltpu.VMEM(sums, F32)] + scratch
        scratch += [pltpu.VMEM((ff // lanes, width, lanes), F32), pltpu.VMEM((ff, width), F32)]
        scratch += [pltpu.VMEM(v.shape, BF16) for v in before] + [pltpu.SemaphoreType.DMA((4,))]
    return pl.pallas_call(
        functools.partial(body, nb, taps, speakers, runs, first, last, each, low),
        out_shape=out_shape,
        grid_spec=pltpu.PrefetchScalarGridSpec(
            num_scalar_prefetch=3, grid=(n,), in_specs=in_specs, out_specs=out_specs, scratch_shapes=scratch),
        cost_estimate=pl.CostEstimate(flops=HINT if last else 0, transcendentals=0, bytes_accessed=0),
        compiler_params=pltpu.CompilerParams(dimension_semantics=("arbitrary",), vmem_limit_bytes=60 << 20),
        name="block",
    )(meta, speaker, counts, *args)


def pack_body(runs, nb, meta_ref, clips, grads, *refs):
    blocks, sems = refs[:-1], refs[-1]
    each = clips.shape[0] // nb
    copies, low, at = [], 0, 0
    for run in runs:
        for d in range(1, nb):
            slot = lax.rem(meta_ref[0] + d, nb) * each + low
            for q, array in enumerate((clips, grads)):
                copies.append(pltpu.make_async_copy(array.at[pl.ds(slot, run)], blocks[at].at[q], sems.at[2 * at + q]))
            at += 1
        low += run
    for copy in copies:
        copy.start()
    for copy in copies:
        copy.wait()


def pack_call(meta, runs, nb, clips, grads):
    length, lanes = clips.shape[1:]
    hbm = pl.BlockSpec(memory_space=pl.ANY)
    sm = pl.BlockSpec(memory_space=pltpu.SMEM)
    vm = pl.BlockSpec(memory_space=pltpu.VMEM)
    blocks = [jax.ShapeDtypeStruct((2, run, length, lanes), BF16) for run in runs for _ in range(1, nb)]
    return pl.pallas_call(
        functools.partial(pack_body, runs, nb),
        out_shape=blocks,
        in_specs=[sm, hbm, hbm],
        out_specs=[vm] * len(blocks),
        scratch_shapes=[pltpu.SemaphoreType.DMA((2 * len(blocks),))],
        name="pack",
    )(meta, clips, grads)


def share_body(taps, speakers, place_ref, w_in, w_out, scale, shift, conv, cb, bo, ls, bi, share, small):
    lanes = share.shape[1]
    small[0:speakers, :] = scale[...].astype(F32)
    small[speakers:2 * speakers, :] = shift[...].astype(F32)
    at = 2 * speakers
    small[at:at + taps, :] = conv[...].astype(F32)
    at += taps
    for v in (cb, bo, ls):
        small[at, :] = v[...].astype(F32)
        at += 1
    tiles = bi.shape[0] // lanes
    for r in range(tiles):
        small[at + r, :] = bi[pl.ds(r * lanes, lanes)].astype(F32)
    at += tiles
    small[at:, :] = jnp.zeros((small.shape[0] - at, lanes), F32)
    ra, rb, rs = w_in.shape[0], w_out.shape[0], small.shape[0] // GROUP
    for r in range(tiles):
        share[r * ra:(r + 1) * ra, :] = w_in[:, r * lanes:(r + 1) * lanes]
    base = tiles * ra
    for r in range(w_out.shape[1] // lanes):
        share[base + r * rb:base + (r + 1) * rb, :] = w_out[:, r * lanes:(r + 1) * lanes]
    base += w_out.shape[1] // lanes * rb
    share[base:base + rs, :] = small[pl.ds(pl.multiple_of(place_ref[1] * rs, rs), rs), :].astype(BF16)


def share_call(place, w_in, w_out, small, small_rows):
    lanes = small[0].shape[1]
    speakers, taps = small[0].shape[0], small[2].shape[0]
    ra, rb = w_in.shape[0] // GROUP, w_out.shape[0] // GROUP
    rows = w_in.shape[1] // lanes * ra + w_out.shape[1] // lanes * rb + small_rows // GROUP
    full = lambda shape: pl.BlockSpec(shape, lambda i, *_: (0,) * len(shape))
    share_row = lambda shape: pl.BlockSpec(shape, lambda i, place: (place[1], 0))
    return pl.pallas_call(
        functools.partial(share_body, taps, speakers),
        out_shape=jax.ShapeDtypeStruct((rows, lanes), BF16),
        grid_spec=pltpu.PrefetchScalarGridSpec(
            num_scalar_prefetch=1, grid=(1,),
            in_specs=[share_row((ra, w_in.shape[1])), share_row((rb, w_out.shape[1]))] + [full(v.shape) for v in small],
            out_specs=full((rows, lanes)),
            scratch_shapes=[pltpu.VMEM((small_rows, lanes), F32)]),
        compiler_params=pltpu.CompilerParams(dimension_semantics=("arbitrary",)),
        name="share",
    )(place, w_in, w_out, *small)


def stack_body(*refs):
    for d, v in enumerate(refs[:-1]):
        refs[-1][d] = v[...]


def stack_call(parts):
    return pl.pallas_call(
        stack_body,
        out_shape=jax.ShapeDtypeStruct((len(parts),) + parts[0].shape, BF16),
        name="gathered",
    )(*parts)


def finish_body(nb, ra, rb, rs, tiles, lanes, taps, speakers, meta_ref, *refs):
    ins = [refs[s % 2].at[s // 2] for s in range(GROUP)]
    g_in, g_out, scale, shift, conv, cb, bo, ls, bi, small = refs[2:]
    for s in range(GROUP):
        part = meta_ref[1] ^ s
        for r in range(tiles):
            g_in[pl.ds(pl.multiple_of(part * ra, ra), ra), r * lanes:(r + 1) * lanes] = ins[s][r * ra:(r + 1) * ra, :].astype(F32)
        base = tiles * ra
        for r in range(nb):
            g_out[pl.ds(pl.multiple_of(part * rb, 16), rb), r * lanes:(r + 1) * lanes] = ins[s][base + r * rb:base + (r + 1) * rb, :].astype(F32)
        base += nb * rb
        small[pl.ds(pl.multiple_of(part * rs, rs), rs), :] = ins[s][base:base + rs, :].astype(F32)
    scale[...] = small[0:speakers, :]
    shift[...] = small[speakers:2 * speakers, :]
    at = 2 * speakers
    conv[...] = small[at:at + taps, :]
    at += taps
    cb[...] = small[at:at + 1, :]
    bo[...] = small[at + 1:at + 2, :]
    ls[...] = small[at + 2:at + 3, :]
    for r in range(tiles):
        bi[pl.ds(r * lanes, lanes)] = small[at + 3 + r, :]


def finish_call(meta, parts, nb, ra, rb, rs, tiles, taps, speakers):
    lanes = parts[0].shape[2]
    vm = pl.BlockSpec(memory_space=pltpu.VMEM)
    sm = pl.BlockSpec(memory_space=pltpu.SMEM)
    shapes = [(nb * lanes, tiles * lanes), (tiles * lanes, nb * lanes), (speakers, lanes), (speakers, lanes), (taps, lanes),
              (1, lanes), (1, lanes), (1, lanes), (tiles * lanes,)]
    return pl.pallas_call(
        functools.partial(finish_body, nb, ra, rb, rs, tiles, lanes, taps, speakers),
        in_specs=[sm] + [vm] * 2,
        out_specs=[vm] * len(shapes),
        out_shape=[jax.ShapeDtypeStruct(s, F32) for s in shapes],
        scratch_shapes=[pltpu.VMEM((rs * GROUP, lanes), F32)],
        name="finish",
    )(meta, *parts)


def ring(axis, size, shift):
    return lambda v: lax.ppermute(v, axis, [(i, (i + shift) % size) for i in range(size)])


def flip(axis, size, mask):
    return lambda v: lax.ppermute(v, axis, [(i, i ^ mask) for i in range(size)])


def gather_group(v, dp_count, gates):
    a, b = flip("dp", dp_count, 2)(v), flip("dp", dp_count, 4)(v)
    a, *one = lax.optimization_barrier((a, *gates[0]))
    near = jnp.stack([v, a, b, flip("dp", dp_count, 4)(a)])
    near, *two = lax.optimization_barrier((near, *gates[1]))
    return [near, flip("dp", dp_count, 1)(near)], (one, two)


def gather_small(v, dp_count):
    near = jnp.stack([v] + [flip("dp", dp_count, 2 * m)(v) for m in range(1, GROUP // 2)])
    return [near, flip("dp", dp_count, 1)(near)]


def per_device(clips_in, speaker, counts, conv_weight, conv_bias, scale_table, shift_table,
               w_in, b_in, w_out, b_out, layer_scale, grad_out):
    clip_num, length, lanes = clips_in.shape
    nb = lax.axis_size("chan")
    dp_count = lax.axis_size("dp")
    me = lax.axis_index("chan")
    dp = lax.axis_index("dp")
    speakers = scale_table.shape[0]
    taps = conv_weight.shape[0]
    per = w_in.shape[1]
    tiles = per // lanes
    width = nb * lanes
    place = dp % GROUP
    sizes = [sum(r) for r in RUNS]
    each = clip_num // nb
    assert each == sum(sizes)
    meta = jnp.stack([me, place]).astype(jnp.int32)

    ra, rb = width // GROUP, per // GROUP
    small = [scale_table, shift_table, conv_weight, conv_bias, b_out, layer_scale, b_in]
    used = 2 * speakers + taps + 3 + tiles
    small_rows = -(-used // (GROUP * 16)) * GROUP * 16
    share = share_call(meta, w_in, w_out, small, small_rows)
    packed = pack_call(meta, sum(RUNS, ()), nb, clips_in, grad_out)

    shares = [share] + [ring("chan", nb, d)(share) for d in range(1, nb)]
    stacked = stack_call(shares)
    stacked, *packed = lax.optimization_barrier((stacked, *packed))
    came = [ring("chan", nb, 1 + j % (nb - 1))(v) for j, v in enumerate(packed)]
    packed = []
    for runs in RUNS:
        packed.append([])
        for _ in runs:
            packed[-1].append(came[:nb - 1])
            came = came[nb - 1:]
    gathered, packed[0] = gather_group(stacked, dp_count, packed[0])

    sums, kept, back, low = None, None, [], 0
    for k, n in enumerate(sizes):
        out = block_call(meta, speaker, counts, low, clips_in, grad_out, packed[k], gathered, nb * per,
                         taps, speakers, small_rows, sums, kept)
        if k:
            keep, send = out[nb:]
        else:
            kept, sums, gathered = out[nb:nb + 4], out[nb + 4], out[nb + 5:]
        sent = out[:nb]
        if k:
            sent, back[0][2] = lax.optimization_barrier((sent, back[0][2]))
        elif GATED:
            sent, packed[1][0][1] = lax.optimization_barrier((sent, packed[1][0][1]))
        back.append([sent[0]] + [ring("chan", nb, -d)(sent[d]) for d in range(1, nb)])
        low += n

    send, *back[0] = lax.optimization_barrier((send, *back[0]))
    got = flip("dp", dp_count, 1)(send)
    total = keep[0].astype(F32) + got[0].astype(F32)
    outward = [(keep[m].astype(F32) + got[m].astype(F32)).astype(BF16) for m in range(1, GROUP // 2)]
    outward, back[0] = lax.optimization_barrier((outward, back[0]))
    for m in range(1, GROUP // 2):
        total = total + flip("dp", dp_count, 2 * m)(outward[m - 1]).astype(F32)
    step = GROUP
    while step < dp_count:
        low = total.astype(BF16)
        total = low.astype(F32) + flip("dp", dp_count, step)(low).astype(F32)
        step *= 2
    total, back[-1] = lax.optimization_barrier((total, back[-1]))
    mine = total[0]
    for d in range(1, nb):
        mine = mine + ring("chan", nb, d)(total[d].astype(BF16)).astype(F32)
    clips_out = jnp.zeros(clips_in.shape, BF16)
    grad_clips = grad_out.astype(F32)
    for k, n in enumerate(sizes):
        for d in range(nb):
            at = (me + d) % nb * each + sum(sizes[:k])
            clips_out = lax.dynamic_update_slice_in_dim(clips_out, back[k][d][0], at, 0)
            g = lax.dynamic_slice_in_dim(grad_out, at, n).astype(F32) + back[k][d][1].astype(F32)
            grad_clips = lax.dynamic_update_slice_in_dim(grad_clips, g, at, 0)
    mine, clips_out, grad_clips = lax.optimization_barrier((mine, clips_out, grad_clips))

    g_in, g_out, g_scale, g_shift, g_conv, g_cb, g_bo, g_ls, g_bi = finish_call(
        meta, gather_small(mine.astype(BF16), dp_count), nb, ra, rb, small_rows // GROUP, tiles, taps, speakers)

    return (clips_out, grad_clips, g_conv, g_cb.reshape(lanes), g_scale, g_shift, g_in, g_bi, g_out,
            g_bo.reshape(lanes), g_ls.reshape(lanes))


def solution(mesh):
    act = P("dp", None, "chan")
    col, vec, row = P(None, "chan"), P("chan"), P("chan", None)
    in_specs = (act, P("dp"), P("dp"), col, vec, col, col, col, vec, row, vec, vec, act)
    out_specs = (act, act, col, vec, col, col, col, vec, row, vec, vec)
    return jax.shard_map(per_device, mesh=mesh, in_specs=in_specs, out_specs=out_specs, check_vma=False)
```

```python
import functools

import jax
import jax.numpy as jnp
from jax import lax
from jax.experimental import pallas as pl
from jax.experimental.pallas import tpu as pltpu
from jax.sharding import PartitionSpec as P

RUNS = ((1, 1), (2,))
GROUP = 8
GATED = True

EPS = 1e-06
ROOT_TWO_PI = 2.5066282746310002
F32 = jnp.float32
BF16 = jnp.bfloat16
PAD = 8
HINT = 1 << 36


def gelu_pair(v):
    z = jnp.abs(v)
    t = 1.0 / (1.0 + (0.3275911 * 0.7071067811865476) * z)
    e = jnp.exp(v * v * -0.5)
    poly = t * (0.5 * 0.254829592 + t * (0.5 * -0.284496736 + t * (0.5 * 1.421413741 + t * (0.5 * -1.453152027 + t * (0.5 * 1.061405429)))))
    tail = poly * e
    cdf = jnp.where(v >= 0.0, 1.0 - tail, tail)
    return v * cdf, cdf + v * (e * (1.0 / ROOT_TWO_PI))


def dot(a, b, ca, cb):
    return lax.dot_general(a, b, (((ca,), (cb,)), ((), ())), preferred_element_type=F32)


class Order:
    def __init__(self, me, count):
        self.me, self.count = me, count

    def __getitem__(self, d):
        return lax.rem(self.me + self.count - d, self.count)


def body(n_blocks, taps, speakers, runs, first, last, each, first_slot,
         meta_ref, spk_ref, count_ref, *refs):
    nb = n_blocks
    order_ref = Order(meta_ref[0], nb)
    x0, g0 = refs[:2]
    k = 2
    p = []
    for _ in runs:
        p.append(refs[k:k + nb - 1])
        k += nb - 1
    if first:
        shares = [refs[k + s % 2].at[s // 2] for s in range(GROUP)]
        k += 2
    else:
        w_in, w_out, prm = refs[k:k + 3]
        k += 3
    if not first:
        got = refs[k]
        k += 1
    if last:
        before = refs[k:k + 4]
        k += 4
    o = refs[k:k + nb]
    k += nb
    if last:
        keep, send = refs[k:k + 2]
        k += 2
        (gwi, gwo, *held, sems) = refs[-7:]
    (nlow_all, blow_all, act_all, plow_all, gsm, *refs) = refs[k:]
    if first:
        w_in, w_out, prm, *refs = refs
    xpad, gpad, normed, gin, slope, wide, b_in = refs[:7]
    i = pl.program_id(0)
    length, lanes = normed.shape[1], normed.shape[2]
    width = nb * lanes
    ff = act_all.shape[2]
    per = ff // nb
    tiles = per // lanes
    margin = taps // 2
    r_conv, r_cb = 2 * speakers, 2 * speakers + taps
    r_bo, r_ls, r_bi = r_cb + 1, r_cb + 2, r_cb + 3
    cols = [pl.multiple_of(order_ref[d] * lanes, lanes) for d in range(nb)]

    @pl.when(i == 0)
    def _():
        for d in range(nb):
            zero = jnp.zeros((PAD, lanes), F32)
            xpad[d, 0:PAD, :] = zero
            xpad[d, PAD + length:, :] = zero
            gpad[d, 0:PAD, :] = zero
            gpad[d, PAD + length:, :] = zero
        gsm[...] = jnp.zeros_like(gsm) if first else got[...]
        if first:
            ra, rb, rs = width // GROUP, per // GROUP, prm.shape[1] // GROUP
            for s in range(GROUP):
                part = meta_ref[1] ^ s

                def unpack(d, carry):
                    c = order_ref[d]
                    for r in range(tiles):
                        w_in[pl.ds(pl.multiple_of(part * ra, ra), ra), pl.ds(pl.multiple_of(c * per + r * lanes, lanes), lanes)] = shares[s][d, r * ra:(r + 1) * ra, :]
                    base = tiles * ra
                    for r in range(nb):
                        w_out[pl.ds(pl.multiple_of(c * per + part * rb, 16), rb), r * lanes:(r + 1) * lanes] = shares[s][d, base + r * rb:base + (r + 1) * rb, :]
                    base += nb * rb
                    prm[d, pl.ds(pl.multiple_of(part * rs, rs), rs), :] = shares[s][d, base:base + rs, :].astype(F32)
                    return carry
                lax.fori_loop(0, nb, unpack, 0)
        for d in range(nb):
            for r in range(tiles):
                at = pl.multiple_of(order_ref[d] * per + r * lanes, lanes)
                b_in[:, pl.ds(at, lanes)] = prm[d, r_bi + r:r_bi + r + 1, :]

        if last:
            for j in range(4):
                pltpu.make_async_copy(before[j], held[j], sems.at[j]).start()

    row = i if last else 0
    nlow, blow, act, plow = (v.at[row] for v in (nlow_all, blow_all, act_all, plow_all))
    xpad[0, PAD:PAD + length, :] = x0[0].astype(F32)
    gin[0] = g0[0]
    low = 0
    for run, part in zip(runs, p):
        @pl.when((i >= low) & (i < low + run))
        def _(low=low, run=run, part=part):
            at = i - low if run > 1 else 0
            for d in range(1, nb):
                xpad[d, PAD:PAD + length, :] = part[d - 1][0, at].astype(F32)
                gin[d] = part[d - 1][1, at]
        low += run

    slot = meta_ref[0] * each + first_slot + i
    spk = spk_ref[slot]
    live = (slot < count_ref[0]).astype(F32)
    total = jnp.zeros((length, 1), F32)
    for d in range(nb):
        acc = jnp.broadcast_to(prm[d, r_cb:r_cb + 1, :], (length, lanes))
        for t in range(taps):
            s = PAD - margin + t
            acc = acc + prm[d, r_conv + t:r_conv + t + 1, :] * xpad[d, s:s + length, :]
        normed[d] = acc
        total = total + jnp.sum(acc, 1, keepdims=True)
    mean = total / width
    square = jnp.zeros((length, 1), F32)
    for d in range(nb):
        c = normed[d] - mean
        normed[d] = c
        square = square + jnp.sum(c * c, 1, keepdims=True)
    inv = lax.rsqrt(square / width + EPS)
    for d in range(nb):
        v = normed[d] * inv
        normed[d] = v
        sc = prm[d, pl.ds(spk, 1), :]
        sh = prm[d, pl.ds(speakers + spk, 1), :]
        nlow[:, pl.ds(cols[d], lanes)] = (v * sc + sh).astype(BF16)

    step = 512
    for f in range(0, ff, step):
        pre = dot(nlow[...], w_in[:, f:f + step], 1, 0) + b_in[:, f:f + step]
        a, s = gelu_pair(pre)
        act[:, f:f + step] = a.astype(BF16)
        slope[:, f:f + step] = s
    wide[...] = dot(act[...], w_out[...], 1, 0)
    for d in range(nb):
        b = wide[:, pl.ds(cols[d], lanes)] + prm[d, r_bo:r_bo + 1, :]
        ls = prm[d, r_ls:r_ls + 1, :] * live
        x = xpad[d, PAD:PAD + length, :]
        g = gin[d].astype(F32)
        o[d][0, 0] = (x + b * ls).astype(BF16)
        gb = g * ls
        gsm[d, r_bo:r_bo + 1, :] += jnp.sum(gb, 0, keepdims=True)
        gsm[d, r_ls:r_ls + 1, :] += jnp.sum(g * b, 0, keepdims=True) * live
        blow[:, pl.ds(cols[d], lanes)] = gb.astype(BF16)
    for f in range(0, ff, step):
        gp = dot(blow[...], w_out[f:f + step, :], 1, 1) * slope[:, f:f + step]
        plow[:, f:f + step] = gp.astype(BF16)
        gsum = jnp.sum(gp, 0, keepdims=True)
        for r in range(step // lanes):
            q = f // lanes + r
            gsm[nb, q:q + 1, :] += gsum[:, r * lanes:(r + 1) * lanes]
    wide[...] = dot(plow[...], w_in[...], 1, 1)
    m1 = jnp.zeros((length, 1), F32)
    m2 = jnp.zeros((length, 1), F32)
    for d in range(nb):
        gn = wide[:, pl.ds(cols[d], lanes)]
        v = normed[d]
        gv = gn * v
        gsm[d, pl.ds(spk, 1), :] += jnp.sum(gv, 0, keepdims=True)
        gsm[d, pl.ds(speakers + spk, 1), :] += jnp.sum(gn, 0, keepdims=True)
        sc = prm[d, pl.ds(spk, 1), :]
        m1 = m1 + jnp.sum(gn * sc, 1, keepdims=True)
        m2 = m2 + jnp.sum(gv * sc, 1, keepdims=True)
    m1 = m1 / width
    m2 = m2 / width
    for d in range(nb):
        sc = prm[d, pl.ds(spk, 1), :]
        gc = (wide[:, pl.ds(cols[d], lanes)] * sc - m1 - normed[d] * m2) * inv
        gpad[d, PAD:PAD + length, :] = gc
        gsm[d, r_cb:r_cb + 1, :] += jnp.sum(gc, 0, keepdims=True)
        acc = jnp.zeros((length, lanes), F32)
        for t in range(taps):
            s = PAD - margin + t
            gsm[d, r_conv + t:r_conv + t + 1, :] += jnp.sum(xpad[d, s:s + length, :] * gc, 0, keepdims=True)
            s = PAD + margin - t
            acc = acc + prm[d, r_conv + t:r_conv + t + 1, :] * gpad[d, s:s + length, :]
        o[d][1, 0] = acc.astype(BF16)

    if last:
        @pl.when(i == pl.num_programs(0) - 1)
        def _():
            for j in range(4):
                pltpu.make_async_copy(before[j], held[j], sems.at[j]).wait()
            flat = [v[...].reshape(-1, v.shape[2]) for v in (nlow_all, blow_all)]
            heads = [v[...].reshape(-1, v.shape[2]) for v in held[:2]]
            for f in range(0, ff, step):
                cut = lambda v: v[:, :, f:f + step].reshape(-1, step)
                da = dot(flat[0], cut(plow_all), 0, 0) + dot(heads[0], cut(held[3]), 0, 0)
                for r in range(step // lanes):
                    gwi[f // lanes + r] = da[:, r * lanes:(r + 1) * lanes]
                gwo[f:f + step, :] = dot(cut(act_all), flat[1], 0, 0) + dot(cut(held[2]), heads[1], 0, 0)
            for d in range(nb):
                for r in range(tiles):
                    gsm[d, r_bi + r:r_bi + r + 1, :] = gsm[nb, pl.ds(order_ref[d] * tiles + r, 1), :]
            place = meta_ref[1]
            ra, rb, rs = width // GROUP, per // GROUP, gsm.shape[1] // GROUP

            def emit(m, carry):
                for e in range(nb):
                    d = -e % nb
                    c = order_ref[d]
                    for out, part in ((keep, place ^ (2 * m)), (send, place ^ (2 * m) ^ 1)):
                        for r in range(tiles):
                            v = gwi[c * tiles + r, pl.ds(pl.multiple_of(part * ra, ra), ra), :]
                            out[m, e, r * ra:(r + 1) * ra, :] = v.astype(out.dtype)
                        base = tiles * ra
                        for r in range(nb):
                            v = gwo[pl.ds(pl.multiple_of(c * per + part * rb, 16), rb), r * lanes:(r + 1) * lanes]
                            out[m, e, base + r * rb:base + (r + 1) * rb, :] = v.astype(out.dtype)
                        base += nb * rb
                        v = gsm[d, pl.ds(pl.multiple_of(part * rs, rs), rs), :]
                        out[m, e, base:base + rs, :] = v.astype(out.dtype)
                return carry
            lax.fori_loop(0, GROUP // 2, emit, 0)


def block_call(meta, speaker, counts, low, clips, grads, packed, shares, ff, taps, speakers, small_rows, carried, before):
    nb = len(packed[0]) + 1
    runs = [part[0].shape[1] for part in packed]
    n = sum(runs)
    each = clips.shape[0] // nb
    _, _, length, lanes = packed[0][0].shape
    width = nb * lanes
    first, last = carried is None, before is not None
    per = ff // nb
    rows = (width // GROUP) * (per // lanes) + (per // GROUP) * nb + small_rows // GROUP
    widths = (width, width, ff, ff)
    full = lambda shape: pl.BlockSpec(shape, lambda i, *_: (0,) * len(shape), pipeline_mode=pl.Buffered(1))
    step = lambda *shape: pl.BlockSpec((1,) + shape, lambda i, *_: (i,) + (0,) * len(shape))
    own = pl.BlockSpec((1, length, lanes), lambda i, meta, *_: (meta[0] * each + low + i, 0, 0))
    sums = (nb + 1, small_rows, lanes)
    args = [clips, grads] + [v for part in packed for v in part] + list(shares)
    in_specs = [own, own] + [full(v.shape) for v in args[2:]]
    out_shape = [jax.ShapeDtypeStruct((2, n, length, lanes), BF16)] * nb
    out_specs = [pl.BlockSpec((2, 1, length, lanes), lambda i, *_: (0, i, 0, 0))] * nb
    if not first:
        args.append(carried)
        in_specs.append(full(sums))
    if last:
        args += list(before)
        in_specs += [pl.BlockSpec(memory_space=pl.ANY)] * 4
        out_shape += [jax.ShapeDtypeStruct((GROUP // 2, nb, rows, lanes), BF16)] * 2
        out_specs += [pl.BlockSpec((GROUP // 2, nb, rows, lanes), lambda i, *_: (0, 0, 0, 0))] * 2
    else:
        out_shape += [jax.ShapeDtypeStruct((n, length, w), BF16) for w in widths] + [jax.ShapeDtypeStruct(sums, F32)]
        out_specs += [step(length, w) for w in widths] + [pl.BlockSpec(sums, lambda i, *_: (0, 0, 0))]
        weights = [((width, ff), BF16), ((ff, width), BF16), ((nb, small_rows, lanes), F32)]
        out_shape += [jax.ShapeDtypeStruct(shape, t) for shape, t in weights]
        out_specs += [full(shape) for shape, _ in weights]
    scratch = [
        pltpu.VMEM((nb, length + 2 * PAD, lanes), F32),
        pltpu.VMEM((nb, length + 2 * PAD, lanes), F32),
        pltpu.VMEM((nb, length, lanes), F32),
        pltpu.VMEM((nb, length, lanes), BF16),
        pltpu.VMEM((length, ff), F32),
        pltpu.VMEM((length, width), F32),
        pltpu.VMEM((1, ff), F32),
    ]
    if last:
        scratch = [pltpu.VMEM((n, length, w), BF16) for w in widths] + [pltpu.VMEM(sums, F32)] + scratch
        scratch += [pltpu.VMEM((ff // lanes, width, lanes), F32), pltpu.VMEM((ff, width), F32)]
        scratch += [pltpu.VMEM(v.shape, BF16) for v in before] + [pltpu.SemaphoreType.DMA((4,))]
    return pl.pallas_call(
        functools.partial(body, nb, taps, speakers, runs, first, last, each, low),
        out_shape=out_shape,
        grid_spec=pltpu.PrefetchScalarGridSpec(
            num_scalar_prefetch=3, grid=(n,), in_specs=in_specs, out_specs=out_specs, scratch_shapes=scratch),
        cost_estimate=pl.CostEstimate(flops=HINT if last else 0, transcendentals=0, bytes_accessed=0),
        compiler_params=pltpu.CompilerParams(dimension_semantics=("arbitrary",), vmem_limit_bytes=60 << 20),
        name="block",
    )(meta, speaker, counts, *args)


def pack_body(runs, nb, meta_ref, clips, grads, *refs):
    blocks, sems = refs[:-1], refs[-1]
    each = clips.shape[0] // nb
    copies, low, at = [], 0, 0
    for run in runs:
        for d in range(1, nb):
            slot = lax.rem(meta_ref[0] + d, nb) * each + low
            for q, array in enumerate((clips, grads)):
                copies.append(pltpu.make_async_copy(array.at[pl.ds(slot, run)], blocks[at].at[q], sems.at[2 * at + q]))
            at += 1
        low += run
    for copy in copies:
        copy.start()
    for copy in copies:
        copy.wait()


def pack_call(meta, runs, nb, clips, grads):
    length, lanes = clips.shape[1:]
    hbm = pl.BlockSpec(memory_space=pl.ANY)
    sm = pl.BlockSpec(memory_space=pltpu.SMEM)
    vm = pl.BlockSpec(memory_space=pltpu.VMEM)
    blocks = [jax.ShapeDtypeStruct((2, run, length, lanes), BF16) for run in runs for _ in range(1, nb)]
    return pl.pallas_call(
        functools.partial(pack_body, runs, nb),
        out_shape=blocks,
        in_specs=[sm, hbm, hbm],
        out_specs=[vm] * len(blocks),
        scratch_shapes=[pltpu.SemaphoreType.DMA((2 * len(blocks),))],
        name="pack",
    )(meta, clips, grads)


def share_body(taps, speakers, place_ref, w_in, w_out, scale, shift, conv, cb, bo, ls, bi, share, small):
    lanes = share.shape[1]
    small[0:speakers, :] = scale[...].astype(F32)
    small[speakers:2 * speakers, :] = shift[...].astype(F32)
    at = 2 * speakers
    small[at:at + taps, :] = conv[...].astype(F32)
    at += taps
    for v in (cb, bo, ls):
        small[at, :] = v[...].astype(F32)
        at += 1
    tiles = bi.shape[0] // lanes
    for r in range(tiles):
        small[at + r, :] = bi[pl.ds(r * lanes, lanes)].astype(F32)
    at += tiles
    small[at:, :] = jnp.zeros((small.shape[0] - at, lanes), F32)
    ra, rb, rs = w_in.shape[0], w_out.shape[0], small.shape[0] // GROUP
    for r in range(tiles):
        share[r * ra:(r + 1) * ra, :] = w_in[:, r * lanes:(r + 1) * lanes]
    base = tiles * ra
    for r in range(w_out.shape[1] // lanes):
        share[base + r * rb:base + (r + 1) * rb, :] = w_out[:, r * lanes:(r + 1) * lanes]
    base += w_out.shape[1] // lanes * rb
    share[base:base + rs, :] = small[pl.ds(pl.multiple_of(place_ref[0] * rs, rs), rs), :].astype(BF16)


def share_call(place, w_in, w_out, small, small_rows):
    lanes = small[0].shape[1]
    speakers, taps = small[0].shape[0], small[2].shape[0]
    ra, rb = w_in.shape[0] // GROUP, w_out.shape[0] // GROUP
    rows = w_in.shape[1] // lanes * ra + w_out.shape[1] // lanes * rb + small_rows // GROUP
    full = lambda shape: pl.BlockSpec(shape, lambda i, *_: (0,) * len(shape))
    share_row = lambda shape: pl.BlockSpec(shape, lambda i, place: (place[0], 0))
    return pl.pallas_call(
        functools.partial(share_body, taps, speakers),
        out_shape=jax.ShapeDtypeStruct((rows, lanes), BF16),
        grid_spec=pltpu.PrefetchScalarGridSpec(
            num_scalar_prefetch=1, grid=(1,),
            in_specs=[share_row((ra, w_in.shape[1])), share_row((rb, w_out.shape[1]))] + [full(v.shape) for v in small],
            out_specs=full((rows, lanes)),
            scratch_shapes=[pltpu.VMEM((small_rows, lanes), F32)]),
        compiler_params=pltpu.CompilerParams(dimension_semantics=("arbitrary",)),
        name="share",
    )(place, w_in, w_out, *small)


def stack_body(*refs):
    out, sems = refs[-2:]
    copies = [pltpu.make_async_copy(v, out.at[d], sems.at[d]) for d, v in enumerate(refs[:-2])]
    for copy in copies:
        copy.start()
    for copy in copies:
        copy.wait()


def stack_call(parts):
    return pl.pallas_call(
        stack_body,
        in_specs=[pl.BlockSpec(memory_space=pl.ANY)] * len(parts),
        out_specs=pl.BlockSpec(memory_space=pltpu.VMEM),
        out_shape=jax.ShapeDtypeStruct((len(parts),) + parts[0].shape, BF16),
        scratch_shapes=[pltpu.SemaphoreType.DMA((len(parts),))],
        name="gathered",
    )(*parts)


def finish_body(nb, ra, rb, rs, tiles, lanes, taps, speakers, meta_ref, *refs):
    ins = [refs[s % 2].at[s // 2] for s in range(GROUP)]
    g_in, g_out, scale, shift, conv, cb, bo, ls, bi, small = refs[2:]
    for s in range(GROUP):
        part = meta_ref[1] ^ s
        for r in range(tiles):
            g_in[pl.ds(pl.multiple_of(part * ra, ra), ra), r * lanes:(r + 1) * lanes] = ins[s][r * ra:(r + 1) * ra, :].astype(F32)
        base = tiles * ra
        for r in range(nb):
            g_out[pl.ds(pl.multiple_of(part * rb, 16), rb), r * lanes:(r + 1) * lanes] = ins[s][base + r * rb:base + (r + 1) * rb, :].astype(F32)
        base += nb * rb
        small[pl.ds(pl.multiple_of(part * rs, rs), rs), :] = ins[s][base:base + rs, :].astype(F32)
    scale[...] = small[0:speakers, :]
    shift[...] = small[speakers:2 * speakers, :]
    at = 2 * speakers
    conv[...] = small[at:at + taps, :]
    at += taps
    cb[...] = small[at:at + 1, :]
    bo[...] = small[at + 1:at + 2, :]
    ls[...] = small[at + 2:at + 3, :]
    for r in range(tiles):
        bi[pl.ds(r * lanes, lanes)] = small[at + 3 + r, :]


def finish_call(meta, parts, nb, ra, rb, rs, tiles, taps, speakers):
    lanes = parts[0].shape[2]
    vm = pl.BlockSpec(memory_space=pltpu.VMEM)
    sm = pl.BlockSpec(memory_space=pltpu.SMEM)
    shapes = [(nb * lanes, tiles * lanes), (tiles * lanes, nb * lanes), (speakers, lanes), (speakers, lanes), (taps, lanes),
              (1, lanes), (1, lanes), (1, lanes), (tiles * lanes,)]
    return pl.pallas_call(
        functools.partial(finish_body, nb, ra, rb, rs, tiles, lanes, taps, speakers),
        in_specs=[sm] + [vm] * 2,
        out_specs=[vm] * len(shapes),
        out_shape=[jax.ShapeDtypeStruct(s, F32) for s in shapes],
        scratch_shapes=[pltpu.VMEM((rs * GROUP, lanes), F32)],
        name="finish",
    )(meta, *parts)


def ring(axis, size, shift):
    return lambda v: lax.ppermute(v, axis, [(i, (i + shift) % size) for i in range(size)])


def flip(axis, size, mask):
    return lambda v: lax.ppermute(v, axis, [(i, i ^ mask) for i in range(size)])


def gather_group(v, dp_count, gates):
    a, b = flip("dp", dp_count, 2)(v), flip("dp", dp_count, 4)(v)
    a, *one = lax.optimization_barrier((a, *gates[0]))
    near = jnp.stack([v, a, b, flip("dp", dp_count, 4)(a)])
    near, *two = lax.optimization_barrier((near, *gates[1]))
    return [near, flip("dp", dp_count, 1)(near)], (one, two)


def gather_small(v, dp_count):
    near = jnp.stack([v] + [flip("dp", dp_count, 2 * m)(v) for m in range(1, GROUP // 2)])
    return [near, flip("dp", dp_count, 1)(near)]


def per_device(clips_in, speaker, counts, conv_weight, conv_bias, scale_table, shift_table,
               w_in, b_in, w_out, b_out, layer_scale, grad_out):
    clip_num, length, lanes = clips_in.shape
    nb = lax.axis_size("chan")
    dp_count = lax.axis_size("dp")
    me = lax.axis_index("chan")
    dp = lax.axis_index("dp")
    speakers = scale_table.shape[0]
    taps = conv_weight.shape[0]
    per = w_in.shape[1]
    tiles = per // lanes
    width = nb * lanes
    place = lax.rem(dp, GROUP)
    sizes = [sum(r) for r in RUNS]
    each = clip_num // nb
    assert each == sum(sizes)
    meta = jnp.stack([me, place]).astype(jnp.int32)

    ra, rb = width // GROUP, per // GROUP
    small = [scale_table, shift_table, conv_weight, conv_bias, b_out, layer_scale, b_in]
    used = 2 * speakers + taps + 3 + tiles
    small_rows = -(-used // (GROUP * 16)) * GROUP * 16
    share = share_call(place.astype(jnp.int32)[None], w_in, w_out, small, small_rows)
    packed = pack_call(meta, sum(RUNS, ()), nb, clips_in, grad_out)

    shares = [share] + [ring("chan", nb, d)(share) for d in range(1, nb)]
    stacked = stack_call(shares)
    stacked, *packed = lax.optimization_barrier((stacked, *packed))
    came = [ring("chan", nb, 1 + j % (nb - 1))(v) for j, v in enumerate(packed)]
    packed = []
    for runs in RUNS:
        packed.append([])
        for _ in runs:
            packed[-1].append(came[:nb - 1])
            came = came[nb - 1:]
    gathered, packed[0] = gather_group(stacked, dp_count, packed[0])

    sums, kept, back, low = None, None, [], 0
    for k, n in enumerate(sizes):
        out = block_call(meta, speaker, counts, low, clips_in, grad_out, packed[k], gathered, nb * per,
                         taps, speakers, small_rows, sums, kept)
        if k:
            keep, send = out[nb:]
        else:
            kept, sums, gathered = out[nb:nb + 4], out[nb + 4], out[nb + 5:]
        sent = out[:nb]
        if k:
            sent, back[0][2] = lax.optimization_barrier((sent, back[0][2]))
        elif GATED:
            sent, packed[1][0][1] = lax.optimization_barrier((sent, packed[1][0][1]))
        back.append([sent[0]] + [ring("chan", nb, -d)(sent[d]) for d in range(1, nb)])
        low += n

    send, *back[0] = lax.optimization_barrier((send, *back[0]))
    got = flip("dp", dp_count, 1)(send)
    total = keep[0].astype(F32) + got[0].astype(F32)
    outward = [(keep[m].astype(F32) + got[m].astype(F32)).astype(BF16) for m in range(1, GROUP // 2)]
    outward, back[0] = lax.optimization_barrier((outward, back[0]))
    for m in range(1, GROUP // 2):
        total = total + flip("dp", dp_count, 2 * m)(outward[m - 1]).astype(F32)
    step = GROUP
    while step < dp_count:
        low = total.astype(BF16)
        total = low.astype(F32) + flip("dp", dp_count, step)(low).astype(F32)
        step *= 2
    total, back[-1] = lax.optimization_barrier((total, back[-1]))
    mine = total[0]
    for d in range(1, nb):
        mine = mine + ring("chan", nb, d)(total[d].astype(BF16)).astype(F32)
    clips_out = jnp.zeros(clips_in.shape, BF16)
    grad_clips = grad_out.astype(F32)
    for k, n in enumerate(sizes):
        for d in range(nb):
            at = (me + d) % nb * each + sum(sizes[:k])
            clips_out = lax.dynamic_update_slice_in_dim(clips_out, back[k][d][0], at, 0)
            g = lax.dynamic_slice_in_dim(grad_out, at, n).astype(F32) + back[k][d][1].astype(F32)
            grad_clips = lax.dynamic_update_slice_in_dim(grad_clips, g, at, 0)
    mine, clips_out, grad_clips = lax.optimization_barrier((mine, clips_out, grad_clips))

    g_in, g_out, g_scale, g_shift, g_conv, g_cb, g_bo, g_ls, g_bi = finish_call(
        meta, gather_small(mine.astype(BF16), dp_count), nb, ra, rb, small_rows // GROUP, tiles, taps, speakers)

    return (clips_out, grad_clips, g_conv, g_cb.reshape(lanes), g_scale, g_shift, g_in, g_bi, g_out,
            g_bo.reshape(lanes), g_ls.reshape(lanes))


def solution(mesh):
    act = P("dp", None, "chan")
    col, vec, row = P(None, "chan"), P("chan"), P("chan", None)
    in_specs = (act, P("dp"), P("dp"), col, vec, col, col, col, vec, row, vec, vec, act)
    out_specs = (act, act, col, vec, col, col, col, vec, row, vec, vec)
    return jax.shard_map(per_device, mesh=mesh, in_specs=in_specs, out_specs=out_specs, check_vma=False)
```

```python
import functools

import jax
import jax.numpy as jnp
from jax import lax
from jax.experimental import pallas as pl
from jax.experimental.pallas import tpu as pltpu
from jax.sharding import PartitionSpec as P

RUNS = ((1, 1), (2,))
GROUP = 8
GATED = True

EPS = 1e-06
ROOT_TWO_PI = 2.5066282746310002
F32 = jnp.float32
BF16 = jnp.bfloat16
PAD = 8
HINT = 1 << 36


def gelu_pair(v):
    z = jnp.abs(v)
    t = 1.0 / (1.0 + (0.3275911 * 0.7071067811865476) * z)
    e = jnp.exp(v * v * -0.5)
    poly = t * (0.5 * 0.254829592 + t * (0.5 * -0.284496736 + t * (0.5 * 1.421413741 + t * (0.5 * -1.453152027 + t * (0.5 * 1.061405429)))))
    tail = poly * e
    cdf = jnp.where(v >= 0.0, 1.0 - tail, tail)
    return v * cdf, cdf + v * (e * (1.0 / ROOT_TWO_PI))


def dot(a, b, ca, cb):
    return lax.dot_general(a, b, (((ca,), (cb,)), ((), ())), preferred_element_type=F32)


class Order:
    def __init__(self, me, count):
        self.me, self.count = me, count

    def __getitem__(self, d):
        return lax.rem(self.me + self.count - d, self.count)


def body(n_blocks, taps, speakers, runs, first, last, each, first_slot,
         meta_ref, spk_ref, count_ref, *refs):
    nb = n_blocks
    order_ref = Order(meta_ref[0], nb)
    x0, g0 = refs[:2]
    k = 2
    p = []
    for _ in runs:
        p.append(refs[k:k + nb - 1])
        k += nb - 1
    if first:
        shares = [refs[k + s % 2].at[s // 2] for s in range(GROUP)]
        k += 2
    else:
        w_in, w_out, prm = refs[k:k + 3]
        k += 3
    if not first:
        got = refs[k]
        k += 1
    if last:
        before = refs[k:k + 4]
        k += 4
    o = refs[k:k + nb]
    k += nb
    if last:
        keep, send = refs[k:k + 2]
        k += 2
        (gwi, gwo, *held, sems) = refs[-7:]
    (nlow_all, blow_all, act_all, plow_all, gsm, *refs) = refs[k:]
    if first:
        w_in, w_out, prm, *refs = refs
    xpad, gpad, normed, gin, slope, wide, b_in = refs[:7]
    i = pl.program_id(0)
    length, lanes = normed.shape[1], normed.shape[2]
    width = nb * lanes
    ff = act_all.shape[2]
    per = ff // nb
    tiles = per // lanes
    margin = taps // 2
    r_conv, r_cb = 2 * speakers, 2 * speakers + taps
    r_bo, r_ls, r_bi = r_cb + 1, r_cb + 2, r_cb + 3
    cols = [pl.multiple_of(order_ref[d] * lanes, lanes) for d in range(nb)]

    @pl.when(i == 0)
    def _():
        for d in range(nb):
            zero = jnp.zeros((PAD, lanes), F32)
            xpad[d, 0:PAD, :] = zero
            xpad[d, PAD + length:, :] = zero
            gpad[d, 0:PAD, :] = zero
            gpad[d, PAD + length:, :] = zero
        gsm[...] = jnp.zeros_like(gsm) if first else got[...]
        if first:
            ra, rb, rs = width // GROUP, per // GROUP, prm.shape[1] // GROUP
            for s in range(GROUP):
                part = meta_ref[1] ^ s

                def unpack(d, carry):
                    c = order_ref[d]
                    for r in range(tiles):
                        w_in[pl.ds(pl.multiple_of(part * ra, ra), ra), pl.ds(pl.multiple_of(c * per + r * lanes, lanes), lanes)] = shares[s][d, r * ra:(r + 1) * ra, :]
                    base = tiles * ra
                    for r in range(nb):
                        w_out[pl.ds(pl.multiple_of(c * per + part * rb, 16), rb), r * lanes:(r + 1) * lanes] = shares[s][d, base + r * rb:base + (r + 1) * rb, :]
                    base += nb * rb
                    prm[d, pl.ds(pl.multiple_of(part * rs, rs), rs), :] = shares[s][d, base:base + rs, :].astype(F32)
                    return carry
                lax.fori_loop(0, nb, unpack, 0)
        for d in range(nb):
            for r in range(tiles):
                at = pl.multiple_of(order_ref[d] * per + r * lanes, lanes)
                b_in[:, pl.ds(at, lanes)] = prm[d, r_bi + r:r_bi + r + 1, :]

        if last:
            for j in range(4):
                pltpu.make_async_copy(before[j], held[j], sems.at[j]).start()

    row = i if last else 0
    nlow, blow, act, plow = (v.at[row] for v in (nlow_all, blow_all, act_all, plow_all))
    xpad[0, PAD:PAD + length, :] = x0[0].astype(F32)
    gin[0] = g0[0]
    low = 0
    for run, part in zip(runs, p):
        @pl.when((i >= low) & (i < low + run))
        def _(low=low, run=run, part=part):
            at = i - low if run > 1 else 0
            for d in range(1, nb):
                xpad[d, PAD:PAD + length, :] = part[d - 1][0, at].astype(F32)
                gin[d] = part[d - 1][1, at]
        low += run

    slot = meta_ref[0] * each + first_slot + i
    spk = spk_ref[slot]
    live = (slot < count_ref[0]).astype(F32)
    total = jnp.zeros((length, 1), F32)
    for d in range(nb):
        acc = jnp.broadcast_to(prm[d, r_cb:r_cb + 1, :], (length, lanes))
        for t in range(taps):
            s = PAD - margin + t
            acc = acc + prm[d, r_conv + t:r_conv + t + 1, :] * xpad[d, s:s + length, :]
        normed[d] = acc
        total = total + jnp.sum(acc, 1, keepdims=True)
    mean = total / width
    square = jnp.zeros((length, 1), F32)
    for d in range(nb):
        c = normed[d] - mean
        normed[d] = c
        square = square + jnp.sum(c * c, 1, keepdims=True)
    inv = lax.rsqrt(square / width + EPS)
    for d in range(nb):
        v = normed[d] * inv
        normed[d] = v
        sc = prm[d, pl.ds(spk, 1), :]
        sh = prm[d, pl.ds(speakers + spk, 1), :]
        nlow[:, pl.ds(cols[d], lanes)] = (v * sc + sh).astype(BF16)

    step = 512
    for f in range(0, ff, step):
        pre = dot(nlow[...], w_in[:, f:f + step], 1, 0) + b_in[:, f:f + step]
        a, s = gelu_pair(pre)
        act[:, f:f + step] = a.astype(BF16)
        slope[:, f:f + step] = s
    wide[...] = dot(act[...], w_out[...], 1, 0)
    for d in range(nb):
        b = wide[:, pl.ds(cols[d], lanes)] + prm[d, r_bo:r_bo + 1, :]
        ls = prm[d, r_ls:r_ls + 1, :] * live
        x = xpad[d, PAD:PAD + length, :]
        g = gin[d].astype(F32)
        o[d][0, 0] = (x + b * ls).astype(BF16)
        gb = g * ls
        gsm[d, r_bo:r_bo + 1, :] += jnp.sum(gb, 0, keepdims=True)
        gsm[d, r_ls:r_ls + 1, :] += jnp.sum(g * b, 0, keepdims=True) * live
        blow[:, pl.ds(cols[d], lanes)] = gb.astype(BF16)
    for f in range(0, ff, step):
        gp = dot(blow[...], w_out[f:f + step, :], 1, 1) * slope[:, f:f + step]
        plow[:, f:f + step] = gp.astype(BF16)
        gsum = jnp.sum(gp, 0, keepdims=True)
        for r in range(step // lanes):
            q = f // lanes + r
            gsm[nb, q:q + 1, :] += gsum[:, r * lanes:(r + 1) * lanes]
    wide[...] = dot(plow[...], w_in[...], 1, 1)
    m1 = jnp.zeros((length, 1), F32)
    m2 = jnp.zeros((length, 1), F32)
    for d in range(nb):
        gn = wide[:, pl.ds(cols[d], lanes)]
        v = normed[d]
        gv = gn * v
        gsm[d, pl.ds(spk, 1), :] += jnp.sum(gv, 0, keepdims=True)
        gsm[d, pl.ds(speakers + spk, 1), :] += jnp.sum(gn, 0, keepdims=True)
        sc = prm[d, pl.ds(spk, 1), :]
        m1 = m1 + jnp.sum(gn * sc, 1, keepdims=True)
        m2 = m2 + jnp.sum(gv * sc, 1, keepdims=True)
    m1 = m1 / width
    m2 = m2 / width
    for d in range(nb):
        sc = prm[d, pl.ds(spk, 1), :]
        gc = (wide[:, pl.ds(cols[d], lanes)] * sc - m1 - normed[d] * m2) * inv
        gpad[d, PAD:PAD + length, :] = gc
        gsm[d, r_cb:r_cb + 1, :] += jnp.sum(gc, 0, keepdims=True)
        acc = jnp.zeros((length, lanes), F32)
        for t in range(taps):
            s = PAD - margin + t
            gsm[d, r_conv + t:r_conv + t + 1, :] += jnp.sum(xpad[d, s:s + length, :] * gc, 0, keepdims=True)
            s = PAD + margin - t
            acc = acc + prm[d, r_conv + t:r_conv + t + 1, :] * gpad[d, s:s + length, :]
        o[d][1, 0] = acc.astype(BF16)

    if last:
        @pl.when(i == pl.num_programs(0) - 1)
        def _():
            for j in range(4):
                pltpu.make_async_copy(before[j], held[j], sems.at[j]).wait()
            flat = [v[...].reshape(-1, v.shape[2]) for v in (nlow_all, blow_all)]
            heads = [v[...].reshape(-1, v.shape[2]) for v in held[:2]]
            for f in range(0, ff, step):
                cut = lambda v: v[:, :, f:f + step].reshape(-1, step)
                da = dot(flat[0], cut(plow_all), 0, 0) + dot(heads[0], cut(held[3]), 0, 0)
                for r in range(step // lanes):
                    gwi[f // lanes + r] = da[:, r * lanes:(r + 1) * lanes]
                gwo[f:f + step, :] = dot(cut(act_all), flat[1], 0, 0) + dot(cut(held[2]), heads[1], 0, 0)
            for d in range(nb):
                for r in range(tiles):
                    gsm[d, r_bi + r:r_bi + r + 1, :] = gsm[nb, pl.ds(order_ref[d] * tiles + r, 1), :]
            place = meta_ref[1]
            ra, rb, rs = width // GROUP, per // GROUP, gsm.shape[1] // GROUP

            def emit(m, carry):
                for e in range(nb):
                    d = -e % nb
                    c = order_ref[d]
                    for out, part in ((keep, place ^ (2 * m)), (send, place ^ (2 * m) ^ 1)):
                        for r in range(tiles):
                            v = gwi[c * tiles + r, pl.ds(pl.multiple_of(part * ra, ra), ra), :]
                            out[m, e, r * ra:(r + 1) * ra, :] = v.astype(out.dtype)
                        base = tiles * ra
                        for r in range(nb):
                            v = gwo[pl.ds(pl.multiple_of(c * per + part * rb, 16), rb), r * lanes:(r + 1) * lanes]
                            out[m, e, base + r * rb:base + (r + 1) * rb, :] = v.astype(out.dtype)
                        base += nb * rb
                        v = gsm[d, pl.ds(pl.multiple_of(part * rs, rs), rs), :]
                        out[m, e, base:base + rs, :] = v.astype(out.dtype)
                return carry
            lax.fori_loop(0, GROUP // 2, emit, 0)


def block_call(meta, speaker, counts, low, clips, grads, packed, shares, ff, taps, speakers, small_rows, carried, before):
    nb = len(packed[0]) + 1
    runs = [part[0].shape[1] for part in packed]
    n = sum(runs)
    each = clips.shape[0] // nb
    _, _, length, lanes = packed[0][0].shape
    width = nb * lanes
    first, last = carried is None, before is not None
    per = ff // nb
    rows = (width // GROUP) * (per // lanes) + (per // GROUP) * nb + small_rows // GROUP
    widths = (width, width, ff, ff)
    full = lambda shape: pl.BlockSpec(shape, lambda i, *_: (0,) * len(shape), pipeline_mode=pl.Buffered(1))
    step = lambda *shape: pl.BlockSpec((1,) + shape, lambda i, *_: (i,) + (0,) * len(shape))
    own = pl.BlockSpec((1, length, lanes), lambda i, meta, *_: (meta[0] * each + low + i, 0, 0))
    sums = (nb + 1, small_rows, lanes)
    args = [clips, grads] + [v for part in packed for v in part] + list(shares)
    in_specs = [own, own] + [full(v.shape) for v in args[2:]]
    out_shape = [jax.ShapeDtypeStruct((2, n, length, lanes), BF16)] * nb
    out_specs = [pl.BlockSpec((2, 1, length, lanes), lambda i, *_: (0, i, 0, 0))] * nb
    if not first:
        args.append(carried)
        in_specs.append(full(sums))
    if last:
        args += list(before)
        in_specs += [pl.BlockSpec(memory_space=pl.ANY)] * 4
        out_shape += [jax.ShapeDtypeStruct((GROUP // 2, nb, rows, lanes), BF16)] * 2
        out_specs += [pl.BlockSpec((GROUP // 2, nb, rows, lanes), lambda i, *_: (0, 0, 0, 0))] * 2
    else:
        out_shape += [jax.ShapeDtypeStruct((n, length, w), BF16) for w in widths] + [jax.ShapeDtypeStruct(sums, F32)]
        out_specs += [step(length, w) for w in widths] + [pl.BlockSpec(sums, lambda i, *_: (0, 0, 0))]
        weights = [((width, ff), BF16), ((ff, width), BF16), ((nb, small_rows, lanes), F32)]
        out_shape += [jax.ShapeDtypeStruct(shape, t) for shape, t in weights]
        out_specs += [full(shape) for shape, _ in weights]
    scratch = [
        pltpu.VMEM((nb, length + 2 * PAD, lanes), F32),
        pltpu.VMEM((nb, length + 2 * PAD, lanes), F32),
        pltpu.VMEM((nb, length, lanes), F32),
        pltpu.VMEM((nb, length, lanes), BF16),
        pltpu.VMEM((length, ff), F32),
        pltpu.VMEM((length, width), F32),
        pltpu.VMEM((1, ff), F32),
    ]
    if last:
        scratch = [pltpu.VMEM((n, length, w), BF16) for w in widths] + [pltpu.VMEM(sums, F32)] + scratch
        scratch += [pltpu.VMEM((ff // lanes, width, lanes), F32), pltpu.VMEM((ff, width), F32)]
        scratch += [pltpu.VMEM(v.shape, BF16) for v in before] + [pltpu.SemaphoreType.DMA((4,))]
    return pl.pallas_call(
        functools.partial(body, nb, taps, speakers, runs, first, last, each, low),
        out_shape=out_shape,
        grid_spec=pltpu.PrefetchScalarGridSpec(
            num_scalar_prefetch=3, grid=(n,), in_specs=in_specs, out_specs=out_specs, scratch_shapes=scratch),
        cost_estimate=pl.CostEstimate(flops=HINT if last else 0, transcendentals=0, bytes_accessed=0),
        compiler_params=pltpu.CompilerParams(dimension_semantics=("arbitrary",), vmem_limit_bytes=60 << 20),
        name="block",
    )(meta, speaker, counts, *args)


def pack_body(runs, nb, meta_ref, clips, grads, *refs):
    blocks, sems = refs[:-1], refs[-1]
    each = clips.shape[0] // nb
    copies, low, at = [], 0, 0
    for run in runs:
        for d in range(1, nb):
            slot = lax.rem(meta_ref[0] + d, nb) * each + low
            for q, array in enumerate((clips, grads)):
                copies.append(pltpu.make_async_copy(array.at[pl.ds(slot, run)], blocks[at].at[q], sems.at[2 * at + q]))
            at += 1
        low += run
    for copy in copies:
        copy.start()
    for copy in copies:
        copy.wait()


def pack_call(meta, runs, nb, clips, grads):
    length, lanes = clips.shape[1:]
    hbm = pl.BlockSpec(memory_space=pl.ANY)
    sm = pl.BlockSpec(memory_space=pltpu.SMEM)
    vm = pl.BlockSpec(memory_space=pltpu.VMEM)
    blocks = [jax.ShapeDtypeStruct((2, run, length, lanes), BF16) for run in runs for _ in range(1, nb)]
    return pl.pallas_call(
        functools.partial(pack_body, runs, nb),
        out_shape=blocks,
        in_specs=[sm, hbm, hbm],
        out_specs=[vm] * len(blocks),
        scratch_shapes=[pltpu.SemaphoreType.DMA((2 * len(blocks),))],
        name="pack",
    )(meta, clips, grads)


def share_body(taps, speakers, place_ref, w_in, w_out, scale, shift, conv, cb, bo, ls, bi, share, small):
    lanes = share.shape[1]
    small[0:speakers, :] = scale[...].astype(F32)
    small[speakers:2 * speakers, :] = shift[...].astype(F32)
    at = 2 * speakers
    small[at:at + taps, :] = conv[...].astype(F32)
    at += taps
    for v in (cb, bo, ls):
        small[at, :] = v[...].astype(F32)
        at += 1
    tiles = bi.shape[0] // lanes
    for r in range(tiles):
        small[at + r, :] = bi[pl.ds(r * lanes, lanes)].astype(F32)
    at += tiles
    small[at:, :] = jnp.zeros((small.shape[0] - at, lanes), F32)
    ra, rb, rs = w_in.shape[0], w_out.shape[0], small.shape[0] // GROUP
    for r in range(tiles):
        share[r * ra:(r + 1) * ra, :] = w_in[:, r * lanes:(r + 1) * lanes]
    base = tiles * ra
    for r in range(w_out.shape[1] // lanes):
        share[base + r * rb:base + (r + 1) * rb, :] = w_out[:, r * lanes:(r + 1) * lanes]
    base += w_out.shape[1] // lanes * rb
    share[base:base + rs, :] = small[pl.ds(pl.multiple_of(place_ref[0] * rs, rs), rs), :].astype(BF16)


def share_call(place, w_in, w_out, small, small_rows):
    lanes = small[0].shape[1]
    speakers, taps = small[0].shape[0], small[2].shape[0]
    ra, rb = w_in.shape[0] // GROUP, w_out.shape[0] // GROUP
    rows = w_in.shape[1] // lanes * ra + w_out.shape[1] // lanes * rb + small_rows // GROUP
    full = lambda shape: pl.BlockSpec(shape, lambda i, *_: (0,) * len(shape))
    share_row = lambda shape: pl.BlockSpec(shape, lambda i, place: (place[0], 0))
    return pl.pallas_call(
        functools.partial(share_body, taps, speakers),
        out_shape=jax.ShapeDtypeStruct((rows, lanes), BF16),
        grid_spec=pltpu.PrefetchScalarGridSpec(
            num_scalar_prefetch=1, grid=(1,),
            in_specs=[share_row((ra, w_in.shape[1])), share_row((rb, w_out.shape[1]))] + [full(v.shape) for v in small],
            out_specs=full((rows, lanes)),
            scratch_shapes=[pltpu.VMEM((small_rows, lanes), F32)]),
        compiler_params=pltpu.CompilerParams(dimension_semantics=("arbitrary",)),
        name="share",
    )(place, w_in, w_out, *small)


def stack_body(*refs):
    out, sems = refs[-2:]
    copies = [pltpu.make_async_copy(v, out.at[d], sems.at[d]) for d, v in enumerate(refs[:-2])]
    for copy in copies:
        copy.start()
    for copy in copies:
        copy.wait()


def stack_call(parts):
    return pl.pallas_call(
        stack_body,
        in_specs=[pl.BlockSpec(memory_space=pl.ANY)] * len(parts),
        out_specs=pl.BlockSpec(memory_space=pltpu.VMEM),
        out_shape=jax.ShapeDtypeStruct((len(parts),) + parts[0].shape, BF16),
        scratch_shapes=[pltpu.SemaphoreType.DMA((len(parts),))],
        name="gathered",
    )(*parts)


def finish_body(nb, ra, rb, rs, tiles, lanes, taps, speakers, meta_ref, *refs):
    ins = [refs[s % 2].at[s // 2] for s in range(GROUP)]
    g_in, g_out, scale, shift, conv, cb, bo, ls, bi, small = refs[2:]
    for s in range(GROUP):
        part = meta_ref[1] ^ s
        for r in range(tiles):
            g_in[pl.ds(pl.multiple_of(part * ra, ra), ra), r * lanes:(r + 1) * lanes] = ins[s][r * ra:(r + 1) * ra, :].astype(F32)
        base = tiles * ra
        for r in range(nb):
            g_out[pl.ds(pl.multiple_of(part * rb, 16), rb), r * lanes:(r + 1) * lanes] = ins[s][base + r * rb:base + (r + 1) * rb, :].astype(F32)
        base += nb * rb
        small[pl.ds(pl.multiple_of(part * rs, rs), rs), :] = ins[s][base:base + rs, :].astype(F32)
    scale[...] = small[0:speakers, :]
    shift[...] = small[speakers:2 * speakers, :]
    at = 2 * speakers
    conv[...] = small[at:at + taps, :]
    at += taps
    cb[...] = small[at:at + 1, :]
    bo[...] = small[at + 1:at + 2, :]
    ls[...] = small[at + 2:at + 3, :]
    for r in range(tiles):
        bi[pl.ds(r * lanes, lanes)] = small[at + 3 + r, :]


def finish_call(meta, parts, nb, ra, rb, rs, tiles, taps, speakers):
    lanes = parts[0].shape[2]
    vm = pl.BlockSpec(memory_space=pltpu.VMEM)
    sm = pl.BlockSpec(memory_space=pltpu.SMEM)
    shapes = [(nb * lanes, tiles * lanes), (tiles * lanes, nb * lanes), (speakers, lanes), (speakers, lanes), (taps, lanes),
              (1, lanes), (1, lanes), (1, lanes), (tiles * lanes,)]
    return pl.pallas_call(
        functools.partial(finish_body, nb, ra, rb, rs, tiles, lanes, taps, speakers),
        in_specs=[sm] + [vm] * 2,
        out_specs=[vm] * len(shapes),
        out_shape=[jax.ShapeDtypeStruct(s, F32) for s in shapes],
        scratch_shapes=[pltpu.VMEM((rs * GROUP, lanes), F32)],
        name="finish",
    )(meta, *parts)


def ring(axis, size, shift):
    return lambda v: lax.ppermute(v, axis, [(i, (i + shift) % size) for i in range(size)])


def flip(axis, size, mask):
    return lambda v: lax.ppermute(v, axis, [(i, i ^ mask) for i in range(size)])


def gather_group(v, dp_count, gates):
    a, b = flip("dp", dp_count, 2)(v), flip("dp", dp_count, 4)(v)
    a, *one = lax.optimization_barrier((a, *gates[0]))
    near = jnp.stack([v, a, b, flip("dp", dp_count, 4)(a)])
    near, *two = lax.optimization_barrier((near, *gates[1]))
    return [near, flip("dp", dp_count, 1)(near)], (one, two)


def gather_small(v, dp_count):
    near = jnp.stack([v] + [flip("dp", dp_count, 2 * m)(v) for m in range(1, GROUP // 2)])
    return [near, flip("dp", dp_count, 1)(near)]


def per_device(clips_in, speaker, counts, conv_weight, conv_bias, scale_table, shift_table,
               w_in, b_in, w_out, b_out, layer_scale, grad_out):
    clip_num, length, lanes = clips_in.shape
    nb = lax.axis_size("chan")
    dp_count = lax.axis_size("dp")
    me = lax.axis_index("chan")
    dp = lax.axis_index("dp")
    speakers = scale_table.shape[0]
    taps = conv_weight.shape[0]
    per = w_in.shape[1]
    tiles = per // lanes
    width = nb * lanes
    place = lax.rem(dp, GROUP)
    sizes = [sum(r) for r in RUNS]
    each = clip_num // nb
    assert each == sum(sizes)
    meta = jnp.stack([me, place]).astype(jnp.int32)

    ra, rb = width // GROUP, per // GROUP
    small = [scale_table, shift_table, conv_weight, conv_bias, b_out, layer_scale, b_in]
    used = 2 * speakers + taps + 3 + tiles
    small_rows = -(-used // (GROUP * 16)) * GROUP * 16
    share = share_call(place.astype(jnp.int32)[None], w_in, w_out, small, small_rows)
    packed = pack_call(meta, sum(RUNS, ()), nb, clips_in, grad_out)

    shares = [share] + [ring("chan", nb, d)(share) for d in range(1, nb)]
    stacked = stack_call(shares)
    stacked, *packed = lax.optimization_barrier((stacked, *packed))
    came = [ring("chan", nb, 1 + j % (nb - 1))(v) for j, v in enumerate(packed)]
    packed = []
    for runs in RUNS:
        packed.append([])
        for _ in runs:
            packed[-1].append(came[:nb - 1])
            came = came[nb - 1:]
    gathered, packed[0] = gather_group(stacked, dp_count, packed[0])

    sums, kept, back, low = None, None, [], 0
    for k, n in enumerate(sizes):
        out = block_call(meta, speaker, counts, low, clips_in, grad_out, packed[k], gathered, nb * per,
                         taps, speakers, small_rows, sums, kept)
        if k:
            keep, send = out[nb:]
        else:
            kept, sums, gathered = out[nb:nb + 4], out[nb + 4], out[nb + 5:]
        sent = out[:nb]
        if k:
            sent, back[0][2] = lax.optimization_barrier((sent, back[0][2]))
        elif GATED:
            sent, packed[1][0][1] = lax.optimization_barrier((sent, packed[1][0][1]))
        back.append([sent[0]] + [ring("chan", nb, -d)(sent[d]) for d in range(1, nb)])
        low += n

    send, *back[0] = lax.optimization_barrier((send, *back[0]))
    got = flip("dp", dp_count, 1)(send)
    total = keep[0].astype(F32) + got[0].astype(F32)
    outward = [(keep[m].astype(F32) + got[m].astype(F32)).astype(BF16) for m in range(1, GROUP // 2)]
    outward, back[0] = lax.optimization_barrier((outward, back[0]))
    for m in range(1, GROUP // 2):
        total = total + flip("dp", dp_count, 2 * m)(outward[m - 1]).astype(F32)
    step = GROUP
    while step < dp_count:
        low = total.astype(BF16)
        total = low.astype(F32) + flip("dp", dp_count, step)(low).astype(F32)
        step *= 2
    total, back[-1] = lax.optimization_barrier((total, back[-1]))
    mine = total[0]
    for d in range(1, nb):
        mine = mine + ring("chan", nb, d)(total[d].astype(BF16)).astype(F32)
    clips_out = jnp.zeros(clips_in.shape, BF16)
    grad_clips = grad_out.astype(F32)
    for k, n in enumerate(sizes):
        for d in range(nb):
            at = (me + d) % nb * each + sum(sizes[:k])
            clips_out = lax.dynamic_update_slice_in_dim(clips_out, back[k][d][0], at, 0)
            g = lax.dynamic_slice_in_dim(grad_out, at, n).astype(F32) + back[k][d][1].astype(F32)
            grad_clips = lax.dynamic_update_slice_in_dim(grad_clips, g, at, 0)
    mine, clips_out = lax.optimization_barrier((mine, clips_out))

    g_in, g_out, g_scale, g_shift, g_conv, g_cb, g_bo, g_ls, g_bi = finish_call(
        meta, gather_small(mine.astype(BF16), dp_count), nb, ra, rb, small_rows // GROUP, tiles, taps, speakers)

    return (clips_out, grad_clips, g_conv, g_cb.reshape(lanes), g_scale, g_shift, g_in, g_bi, g_out,
            g_bo.reshape(lanes), g_ls.reshape(lanes))


def solution(mesh):
    act = P("dp", None, "chan")
    col, vec, row = P(None, "chan"), P("chan"), P("chan", None)
    in_specs = (act, P("dp"), P("dp"), col, vec, col, col, col, vec, row, vec, vec, act)
    out_specs = (act, act, col, vec, col, col, col, vec, row, vec, vec)
    return jax.shard_map(per_device, mesh=mesh, in_specs=in_specs, out_specs=out_specs, check_vma=False)
```
